256 devices in a mesh: sub: 64 (over x, z, core), crs: 4 (over y).
Axes of the slice: x: 4, y: 4, z: 8, core: 2. Of those that a mesh axis runs over, the one named last changes fastest.
Arguments:
- residual: float32 [256, 6, 3072], P('sub', None, 'crs'), may hold values from -6 to 6
- stiffness: float32 [256, 6, 3072], P('sub', None, 'crs'), may hold values from 0.1 to 10
- solid: int32 [256, 6, 16], P('sub', None, 'crs'), may hold values 0 or 1
- inverses: bfloat16 [256, 6, 192, 3072], P('sub', None, None, 'crs')
- coarse_basis: bfloat16 [256, 24, 6, 3072], P('sub', None, None, 'crs'), may hold values from -0.29882812 to 0.29882812
- assign: int32 [256], replicated, may hold values from 0 to 255, as said below
- corners: int32 [256, 8], P('sub'), may hold values from 0 to 255, as said below
- coarse_inverse: float32 [768, 768], P('crs')
Outputs:
- preconditioned: float32 [256, 6, 3072], P('sub', None, 'crs')
- inner_value: float32 [1], replicated
The draws below stay inside these ranges and needn't reach their ends.
Inputs may be any that keep to these rules, and one draw needn't show every extreme that they name: assign is a permutation of the 256 subdomain numbers, set at run time by the load balancer, so a subdomain's neighbours may be held on any devices. corners[t, c] is the number of corner c = 4 cx + 2 cy + cz of subdomain assign[t], the grid vertex at its place plus (cx, cy, cz) taken periodically, under one fixed permutation of the 256 vertices.
All inputs are finite; a program needn't handle non-finite values. No bound on the sum of `solid` on one device may be relied on, other than what follows from the above.
Results may differ from the reference program's by a relative error of at most 0.0028.
Values sent between devices are 32-bit elements; how exact they have to be, the bound alone decides.
No kernel may reach another device: no remote copies, remote signals or barrier semaphores. Data moves between devices by JAX's collectives and lax.ppermute only.
A program may use at most 128 MiB of HBM per device.

```python
import math
import jax
import jax.numpy as jnp
from jax import lax

PATCHES = 16
K = 192
NPRIM = 24
SUBS = 256
NC = 768


def layout_tables(key):
    order = jax.random.permutation(jax.random.fold_in(key, 11), SUBS).astype(jnp.int32)
    relabel = jax.random.permutation(jax.random.fold_in(key, 12), SUBS).astype(jnp.int32)
    return (order, relabel)


def draw_assign(key, part):
    return layout_tables(key)[0]


def draw_corners(key, part):
    order, relabel = layout_tables(key)
    depth = SUBS // 16
    coord_a = order // (4 * depth)
    coord_b = order // depth % 4
    coord_c = order % depth
    listed = []
    for corner in range(8):
        step_a = corner // 4
        step_b = corner // 2 % 2
        step_c = corner % 2
        vertex = ((coord_a + step_a) % 4 * 4 + (coord_b + step_b) % 4) * depth + (coord_c + step_c) % depth
        listed.append(relabel[vertex])
    return jnp.stack(listed, axis=1).astype(jnp.int32)


def draw_inverses(key, part):
    diag_key = jax.random.fold_in(key, 21)
    off_key = jax.random.fold_in(key, 22)
    diagonal = jnp.exp(jax.random.uniform(diag_key, (SUBS, 6, PATCHES, K), jnp.float32, 0.0, 0.7))
    spread = jax.random.normal(off_key, (SUBS, 6, PATCHES, K, K), jnp.float32) * (0.4 / K ** 0.5)
    identity = jnp.eye(K, dtype=jnp.float32)
    blocks = spread + identity * diagonal[..., None]
    return blocks.transpose(0, 1, 3, 2, 4).reshape(SUBS, 6, K, PATCHES * K).astype(jnp.bfloat16)


def draw_coarse_inverse(key, part):
    diag_key = jax.random.fold_in(key, 31)
    off_key = jax.random.fold_in(key, 32)
    diagonal = jnp.exp(jax.random.uniform(diag_key, (NC,), jnp.float32, -3.5, -2.3))
    spread = jax.random.normal(off_key, (NC, NC), jnp.float32) * (0.05 / NC ** 0.5)
    identity = jnp.eye(NC, dtype=jnp.float32)
    return spread + identity * diagonal[None, :]


def touch_ends(result, rng, low, top_value):
    longest = result.shape.index(max(result.shape))
    spots = []
    for shift in (0, 1):
        where = [jax.random.randint(jax.random.fold_in(rng, axis), (), 0, length) for axis, length in enumerate(result.shape)]
        where[longest] = (where[longest] + shift) % result.shape[longest]
        spots.append(tuple(where))
    return result.at[spots[0]].set(low).at[spots[1]].set(top_value)


def level_of(stream_key, extent, pieces, low, largest):
    gain = 1.0
    for axis_at, blocks in pieces:
        steps = jax.random.uniform(jax.random.fold_in(jax.random.fold_in(stream_key, 6), axis_at), (blocks,), jnp.float32, low / len(pieces), largest / len(pieces))
        gain = gain * jnp.repeat(jnp.exp(steps), extent[axis_at] // blocks).reshape((-1,) + (1,) * (len(extent) - 1 - axis_at))
    return gain


def noise(own_key, shape, scale, bound, pieces=(), held_as=jnp.bfloat16):
    entries = scale * jax.random.normal(own_key, shape, jnp.float32)
    if pieces:
        entries = entries * level_of(own_key, shape, pieces, -0.22, 0.18)
    return jnp.clip(entries, -bound, bound).astype(held_as)


def setup_inputs(seed: int = 0) -> dict:
    splits = jax.random.split(jax.random.key(seed), 9)
    residual = noise(splits[0], (SUBS, 6, PATCHES * K), 1.0, 6.0, ((0, 64), (2, 4)), jnp.float32)
    stiffness = jnp.clip(jnp.exp(math.log(10.0) - 4.6051702 * jax.random.uniform(splits[1], (SUBS, 6, PATCHES * K), jnp.float32) ** level_of(splits[1], (SUBS, 6, PATCHES * K), ((0, 64), (2, 4)), -0.2, 0.2)), 0.1, 10.0)
    solid = touch_ends((jax.random.randint(splits[2], (SUBS, 6, PATCHES), 0, 4) < 3).astype(jnp.int32), jax.random.fold_in(splits[2], 1), 0, 1)
    inverses = draw_inverses(jax.random.fold_in(splits[8], 71), 0)
    coarse_basis = noise(splits[4], (SUBS, NPRIM, 6, PATCHES * K), 0.05, 0.29882812, ((0, 64), (3, 4)))
    assign = draw_assign(jax.random.fold_in(splits[8], 71), 0)
    corners = draw_corners(jax.random.fold_in(splits[8], 71), 0)
    coarse_inverse = draw_coarse_inverse(jax.random.fold_in(splits[8], 71), 0)
    return dict(residual=residual, stiffness=stiffness, solid=solid, inverses=inverses, coarse_basis=coarse_basis, assign=assign, corners=corners, coarse_inverse=coarse_inverse)


def partner_rows(assign, subs):
    depth = subs // 16
    slots = jnp.arange(subs, dtype=jnp.int32)
    inverse = jnp.sum(slots[:, None] * (assign[:, None] == slots[None, :]).astype(jnp.int32), axis=0)
    coord_a = assign // (4 * depth)
    coord_b = (assign // depth) % 4
    coord_c = assign % depth

    def number(first, second, third):
        return (first * 4 + second) * depth + third

    neighbours = jnp.stack([
        number((coord_a + 1) % 4, coord_b, coord_c),
        number(coord_a, (coord_b + 1) % 4, coord_c),
        number(coord_a, coord_b, (coord_c + 1) % depth),
        number((coord_a + 3) % 4, coord_b, coord_c),
        number(coord_a, (coord_b + 3) % 4, coord_c),
        number(coord_a, coord_b, (coord_c + depth - 1) % depth)], axis=1)
    partner_slot = inverse[neighbours]
    partner_face = jnp.array([3, 4, 5, 0, 1, 2], dtype=jnp.int32)
    return (partner_slot * 6 + partner_face[None, :]).reshape(-1).astype(jnp.int32)


def reference(residual, stiffness, solid, inverses, coarse_basis, assign, corners, coarse_inverse):
    subs = residual.shape[0]
    rows = partner_rows(assign, subs)
    flat_r = residual.reshape(subs * 6, -1)
    flat_k = stiffness.reshape(subs * 6, -1)
    partner_r = flat_r[rows]
    partner_k = flat_k[rows]
    weight = flat_k / (flat_k + partner_k)
    weight_partner = partner_k / (flat_k + partner_k)
    solid_f = jnp.repeat(solid.astype(jnp.float32), K, axis=2)
    restricted = (solid_f * (weight * (flat_r + partner_r)).reshape(residual.shape)).astype(jnp.bfloat16)

    def solve_one(pair):
        blocks = pair[0].astype(jnp.float32).reshape(6, K, PATCHES, K)
        vector = pair[1].astype(jnp.float32).reshape(6, PATCHES, K)
        return jnp.einsum('fipj,fpj->fpi', blocks, vector).reshape(6, PATCHES * K)

    local = lax.map(solve_one, (inverses, restricted))
    coarse_part = jnp.einsum('scfk,sfk->sc', coarse_basis.astype(jnp.float32), restricted.astype(jnp.float32))
    index = (3 * corners[:, :, None] + jnp.arange(3, dtype=jnp.int32)[None, None, :]).reshape(subs, 24)
    coarse_residual = jnp.zeros((3 * subs,), jnp.float32).at[index.reshape(-1)].add(coarse_part.reshape(-1))
    coarse_solution = jnp.dot(coarse_residual, coarse_inverse, precision=lax.Precision.HIGHEST)
    corner_values = coarse_solution[index].astype(jnp.bfloat16)
    correction = jnp.einsum('sc,scfk->sfk', corner_values.astype(jnp.float32), coarse_basis.astype(jnp.float32))
    solution = solid_f * (local + correction)
    flat_u = solution.reshape(subs * 6, -1)
    preconditioned = (weight * flat_u + weight_partner * flat_u[rows]).reshape(residual.shape)
    inner_value = jnp.sum(residual * preconditioned).reshape(1)
    return preconditioned, inner_value
```

```python
import jax
import jax.numpy as jnp
from jax import lax
from jax.experimental import pallas as pl
from jax.experimental.pallas import tpu as pltpu
from jax.sharding import PartitionSpec as P


F32 = jnp.float32
BF16 = jnp.bfloat16
VMEM = pltpu.VMEM
SMEM = pltpu.SMEM


def iota(shape, axis):
    return lax.broadcasted_iota(jnp.int32, shape, axis)


def pair_transpose(first, second):
    both = jnp.concatenate([first, second], axis=1)
    turned = both.T
    return turned[:64], turned[64:]


def stack_rows(faces, k):
    return jnp.concatenate(
        [
            faces[s][:, p * 192 + k * 64 : p * 192 + k * 64 + 64]
            for s in range(4)
            for p in range(4)
        ],
        axis=0,
    )


def slot_faces(ref, s, pads):
    return jnp.concatenate([ref[f, s : s + 1, :] for f in range(6)] + pads, axis=0)


def unpack_faces(tiles):
    first = jnp.concatenate([tiles[0], tiles[1]], axis=0).T
    second = jnp.concatenate([tiles[2], jnp.zeros_like(tiles[2])], axis=0).T
    faces = []
    for s in range(4):
        pieces = []
        for p in range(4):
            row = s * 32 + p * 8
            pieces += [first[row : row + 8], second[row : row + 8, :64]]
        faces.append(jnp.concatenate(pieces, axis=1))
    return faces


def to_slots(tiles):
    pad = jnp.zeros((64, 32), F32)
    return jnp.concatenate(
        [
            jnp.concatenate([tile[:, s * 32 : s * 32 + 32] for tile in tiles] + [pad], axis=1)
            for s in range(4)
        ],
        axis=0,
    )


def from_slots(rows, k):
    return jnp.concatenate(
        [rows[s * 64 : s * 64 + 64, k * 32 : k * 32 + 32] for s in range(4)], axis=1
    )


def select_rows(onehot, values):
    high = values.astype(BF16)
    rest = values - high.astype(F32)
    middle = rest.astype(BF16)
    low = (rest - middle.astype(F32)).astype(BF16)
    width = values.shape[1]
    parts = jnp.concatenate([high, middle, low], axis=1)
    out = jnp.dot(onehot, parts, preferred_element_type=F32)
    return (out[:, :width] + out[:, width : 2 * width]) + out[:, 2 * width :]


def rows_ahead(values, count):
    return pltpu.roll(values, (-count) % 256, 0)


def lanes_ahead(values, count):
    return pltpu.roll(values, (-count) % values.shape[1], 1)


def step_forward(values, direction):
    row = iota(values.shape, 0)
    if direction == 0:
        return rows_ahead(values, 64)
    if direction == 1:
        return jnp.where(row // 16 % 4 == 3, rows_ahead(values, -48), rows_ahead(values, 16))
    return jnp.where(row % 16 == 15, rows_ahead(values, -15), rows_ahead(values, 1))


def step_back(values, direction):
    row = iota(values.shape, 0)
    if direction == 0:
        return rows_ahead(values, -64)
    if direction == 1:
        return jnp.where(row // 16 % 4 == 0, rows_ahead(values, 48), rows_ahead(values, -16))
    return jnp.where(row % 16 == 0, rows_ahead(values, 15), rows_ahead(values, -1))


def partner(values):
    face = iota(values.shape, 1) % 8
    minus = lanes_ahead(values, 3)
    plus = lanes_ahead(values, -3)
    out = step_forward(minus, 0)
    out = jnp.where(face == 1, step_forward(minus, 1), out)
    out = jnp.where(face == 2, step_forward(minus, 2), out)
    out = jnp.where(face == 3, step_back(plus, 0), out)
    out = jnp.where(face == 4, step_back(plus, 1), out)
    return jnp.where(face == 5, step_back(plus, 2), out)


def pack_kernel(assign_ref, corners_ref, residual_ref, stiffness_ref, out_ref):
    res = []
    stiff = []
    ones = jnp.ones((1, 768), F32)
    for s in range(4):
        vertex = jnp.full((1, 768), corners_ref[s, 0].astype(F32), F32)
        place = jnp.full((1, 768), assign_ref[s].astype(F32), F32)
        res.append(slot_faces(residual_ref, s, [vertex, place]))
        stiff.append(slot_faces(stiffness_ref, s, [ones, ones]))
    pairs = [((res, 0), (res, 1)), ((res, 2), (stiff, 0)), ((stiff, 1), (stiff, 2))]
    for at, (one, two) in enumerate(pairs):
        a, b = pair_transpose(stack_rows(*one), stack_rows(*two))
        out_ref[:, 0, at * 256 : at * 256 + 128] = a
        out_ref[:, 0, at * 256 + 128 : at * 256 + 256] = b


def weigh_kernel(in_ref, out_ref, weight_ref, weight_partner_ref, place_ref, slot_ref, vertex_ref):
    tiles = [in_ref[:, 0, at * 128 : at * 128 + 128] for at in range(6)]
    res = to_slots(tiles[:3])
    stiff = to_slots(tiles[3:])
    lane = iota((256, 256), 1).astype(F32)
    to_place = jnp.where(res[:, 7:8] == lane, 1.0, 0.0).astype(F32)
    from_place = to_place.astype(BF16)
    to_place = to_place.T.astype(BF16)
    both = select_rows(to_place, jnp.concatenate([res, stiff], axis=1))
    res = both[:, :128]
    stiff = both[:, 128:]
    vertex = jnp.broadcast_to(res[:, 6:7], (256, 128)).T[0:1, :]
    entry_vertex = (iota((768, 1), 0) // 3).astype(F32)
    stiff_partner = partner(stiff)
    total = stiff + stiff_partner
    weight = stiff / total
    back = select_rows(from_place, weight * (res + partner(res)))
    for k in range(3):
        out_ref[:, 0, k * 128 : k * 128 + 128] = from_slots(back, k)
    weight_ref[...] = weight
    weight_partner_ref[...] = stiff_partner / total
    place_ref[...] = to_place
    slot_ref[...] = from_place
    vertex_ref[...] = jnp.where(entry_vertex == vertex, 1.0, 0.0).astype(BF16)


def face_mask(shape, index):
    lane = iota(shape, 1)
    return (lane // 32 == index // 6) & (lane % 8 == index % 6)


def solve_kernel(group, in_ref, solid_ref, inverses_ref, basis_ref, local_ref, message_ref, rhs, total):
    step = pl.program_id(0)
    tiles = [in_ref[:, 0, k * 128 : k * 128 + 128] for k in range(3)]

    @pl.when(step == 0)
    def _():
        patch = iota((64, 128), 1) // 8 % 4
        for k in range(3):
            value = tiles[k] * solid_ref[...]
            for p in range(4):
                row = p * 192 + k * 64
                rhs[row : row + 64, :] = jnp.where(patch == p, value, 0.0).astype(BF16)
        total[...] = jnp.zeros_like(total)

    product = jnp.dot(inverses_ref[...], rhs[...], preferred_element_type=F32)
    held = total[...]
    for at in range(group):
        mask = face_mask((192, 128), step * group + at)
        held = jnp.where(mask, product[at * 192 : at * 192 + 192], held)
    total[...] = held

    @pl.when(step == pl.num_programs(0) - 1)
    def _():
        coarse = jnp.dot(basis_ref[...], rhs[...], preferred_element_type=F32)
        parts = []
        for s in range(4):
            part = jnp.zeros((24, 128), F32)
            for f in range(6):
                at = s * 6 + f
                part = part + jnp.where(
                    face_mask((24, 128), at), coarse[at * 24 : at * 24 + 24], 0.0
                )
            parts += [part, jnp.zeros((8, 128), F32)]
        row = jnp.sum(jnp.concatenate(parts, axis=0).T, axis=0, keepdims=True)
        product_sum = jnp.zeros((64, 128), F32)
        for k in range(3):
            product_sum = product_sum + tiles[k] * held[k * 64 : k * 64 + 64]
        inner = jnp.sum(
            jnp.sum(product_sum, axis=0, keepdims=True) * solid_ref[...], axis=1, keepdims=True
        )
        row = jnp.where(iota((1, 128), 1) == 24, inner, row)
        message_ref[...] = jnp.broadcast_to(row.reshape(1, 1, 128), message_ref.shape)
        local_ref[...] = held


def coarse_kernel(
    corners_ref, in_ref, place_ref, vertex_ref, inverse_ref, basis_ref, local_ref, solid_ref,
    out_ref, inner_ref,
):
    summed = in_ref[0:64, 0, :]
    for y in range(1, 4):
        summed = summed + in_ref[y * 64 : y * 64 + 64, 0, :]
    inner = jnp.sum(jnp.sum(summed, axis=0, keepdims=True)[:, 24:25], axis=1, keepdims=True)
    pad = jnp.zeros((64, 96), F32)
    parts = jnp.concatenate(
        [jnp.concatenate([summed[:, s * 32 : s * 32 + 32], pad], axis=1) for s in range(4)], axis=0
    )
    parts = select_rows(place_ref[...], parts)
    for direction, count in ((2, 3), (1, 6), (0, 12)):
        parts = parts + step_back(lanes_ahead(parts, count), direction)
    by_entry = select_rows(vertex_ref[...], parts)
    own = iota((768, 128), 0) % 3 == iota((768, 128), 1)
    column = jnp.sum(jnp.where(own, by_entry, 0.0), axis=1, keepdims=True)
    solution = jnp.sum(inverse_ref[...] * column, axis=0, keepdims=True)
    diagonal = iota((768, 768), 0) == iota((768, 768), 1)
    residual = jnp.sum(jnp.where(diagonal, column, 0.0), axis=0, keepdims=True)
    rounded = solution.astype(BF16).astype(F32)
    inner_ref[...] = inner + jnp.sum(rounded * residual, axis=1, keepdims=True)
    entry = iota((24, 768), 0)
    lane = iota((24, 768), 1)
    faces = []
    for s in range(4):
        index = entry % 3
        for c in range(8):
            index = jnp.where(entry // 3 == c, entry % 3 + 3 * corners_ref[s, c], index)
        values = jnp.sum(jnp.where(lane == index, rounded, 0.0), axis=1, keepdims=True)
        rows = []
        for f in range(6):
            block = basis_ref[(s * 6 + f) * 24 : (s * 6 + f) * 24 + 24, :].astype(F32)
            rows.append(jnp.sum(block * values, axis=0, keepdims=True))
        faces.append(jnp.concatenate(rows + [jnp.zeros((2, 768), F32)], axis=0))
    a, b = pair_transpose(stack_rows(faces, 0), stack_rows(faces, 1))
    c, _ = pair_transpose(stack_rows(faces, 2), jnp.zeros((128, 64), F32))
    for k, tile in enumerate((a, b, c)):
        out_ref[:, 0, k * 128 : k * 128 + 128] = solid_ref[...] * (
            local_ref[k * 64 : k * 64 + 64] + tile
        )


def average_kernel(in_ref, place_ref, slot_ref, weight_ref, weight_partner_ref, out_ref):
    tiles = [in_ref[:, 0, k * 128 : k * 128 + 128] for k in range(3)]
    values = select_rows(place_ref[...], to_slots(tiles))
    values = weight_ref[...] * values + weight_partner_ref[...] * partner(values)
    back = select_rows(slot_ref[...], values)
    for k in range(3):
        out_ref[:, 0, k * 128 : k * 128 + 128] = from_slots(back, k)


def unpack_kernel(in_ref, out_ref):
    faces = unpack_faces([in_ref[:, 0, k * 128 : k * 128 + 128] for k in range(3)])
    for f in range(6):
        out_ref[f] = jnp.concatenate([faces[s][f : f + 1, :] for s in range(4)], axis=0)


def spec(space=VMEM):
    return pl.BlockSpec(memory_space=space)


def shaped(*shape, dtype=F32):
    return jax.ShapeDtypeStruct(shape, dtype)


def call(kernel, inputs, outputs, name):
    return pl.pallas_call(
        kernel,
        in_specs=[spec(space) for space in inputs],
        out_specs=tuple(spec() for _ in outputs),
        out_shape=tuple(outputs),
        name=name,
        compiler_params=pltpu.CompilerParams(vmem_limit_bytes=24 * 2**20),
    )


def exchange(values, axes):
    return lax.all_to_all(values, axes, 0, 0)


def body(residual, stiffness, solid, inverses, coarse_basis, assign, corners, coarse_inverse):
    full_inverse = lax.all_gather(coarse_inverse, "crs", axis=0, tiled=True)
    mine = lax.dynamic_slice_in_dim(assign, 4 * lax.axis_index("sub"), 4)
    solid_row = jnp.pad(
        solid.transpose(0, 2, 1).astype(F32), ((0, 0), (0, 0), (0, 2))
    ).reshape(1, 128)
    basis_rows = coarse_basis.transpose(0, 2, 1, 3).reshape(576, 768)

    (packed,) = call(pack_kernel, [SMEM, SMEM, VMEM, VMEM], [shaped(64, 1, 768)], "pack")(
        mine, corners, residual.transpose(1, 0, 2), stiffness.transpose(1, 0, 2)
    )
    weighed, weight, weight_partner, to_place, from_place, to_vertex = call(
        weigh_kernel,
        [VMEM],
        [shaped(64, 1, 384), shaped(256, 128), shaped(256, 128)]
        + [shaped(n, 256, dtype=BF16) for n in (256, 256, 768)],
        "weigh",
    )(exchange(packed, "sub"))

    group = 4
    local, message = pl.pallas_call(
        lambda *refs: solve_kernel(group, *refs),
        grid=(24 // group,),
        in_specs=[
            pl.BlockSpec((64, 1, 384), lambda i: (0, 0, 0)),
            pl.BlockSpec((1, 128), lambda i: (0, 0)),
            pl.BlockSpec((group * 192, 768), lambda i: (i, 0)),
            pl.BlockSpec((576, 768), lambda i: (0, 0)),
        ],
        out_specs=(
            pl.BlockSpec((192, 128), lambda i: (0, 0)),
            pl.BlockSpec((256, 1, 128), lambda i: (0, 0, 0)),
        ),
        out_shape=(shaped(192, 128), shaped(256, 1, 128)),
        scratch_shapes=[pltpu.VMEM((768, 128), BF16), pltpu.VMEM((192, 128), F32)],
        name="solve",
        compiler_params=pltpu.CompilerParams(vmem_limit_bytes=24 * 2**20),
    )(exchange(weighed, "sub"), solid_row, inverses.reshape(4608, 768), basis_rows)

    solved, inner = call(
        coarse_kernel,
        [SMEM] + [VMEM] * 7,
        [shaped(64, 1, 384), shaped(1, 1)],
        "coarse",
    )(
        corners,
        exchange(message, ("crs", "sub")),
        to_place,
        to_vertex,
        full_inverse,
        basis_rows,
        local,
        solid_row,
    )
    (averaged,) = call(average_kernel, [VMEM] * 5, [shaped(64, 1, 384)], "average")(
        exchange(solved, "sub"), to_place, from_place, weight, weight_partner
    )
    (out,) = call(unpack_kernel, [VMEM], [shaped(6, 4, 768)], "unpack")(exchange(averaged, "sub"))
    return out.transpose(1, 0, 2), inner.reshape(1)


def solution(mesh):
    return jax.shard_map(
        body,
        mesh=mesh,
        in_specs=(
            P("sub", None, "crs"),
            P("sub", None, "crs"),
            P("sub", None, "crs"),
            P("sub", None, None, "crs"),
            P("sub", None, None, "crs"),
            P(),
            P("sub", None),
            P("crs", None),
        ),
        out_specs=(P("sub", None, "crs"), P()),
        check_vma=False,
    )
```

```python
import jax
import jax.numpy as jnp
from jax import lax
from jax.experimental import pallas as pl
from jax.experimental.pallas import tpu as pltpu
from jax.sharding import PartitionSpec as P


F32 = jnp.float32
BF16 = jnp.bfloat16
VMEM = pltpu.VMEM
SMEM = pltpu.SMEM
HBM = pltpu.HBM


def iota(shape, axis):
    return lax.broadcasted_iota(jnp.int32, shape, axis)


def pair_transpose(first, second):
    both = jnp.concatenate([first, second], axis=1)
    turned = both.T
    return turned[:64], turned[64:]


def stack_rows(faces, k):
    return jnp.concatenate(
        [
            faces[s][:, p * 192 + k * 64 : p * 192 + k * 64 + 64]
            for s in range(4)
            for p in range(4)
        ],
        axis=0,
    )


def slot_faces(ref, s, pads):
    return jnp.concatenate([ref[f, s : s + 1, :] for f in range(6)] + pads, axis=0)


def unpack_faces(tiles):
    first = jnp.concatenate([tiles[0], tiles[1]], axis=0).T
    second = jnp.concatenate([tiles[2], jnp.zeros_like(tiles[2])], axis=0).T
    faces = []
    for s in range(4):
        pieces = []
        for p in range(4):
            row = s * 32 + p * 8
            pieces += [first[row : row + 8], second[row : row + 8, :64]]
        faces.append(jnp.concatenate(pieces, axis=1))
    return faces


def to_slots(tiles):
    pad = jnp.zeros((64, 32), F32)
    return jnp.concatenate(
        [
            jnp.concatenate([tile[:, s * 32 : s * 32 + 32] for tile in tiles] + [pad], axis=1)
            for s in range(4)
        ],
        axis=0,
    )


def from_slots(rows, k):
    return jnp.concatenate(
        [rows[s * 64 : s * 64 + 64, k * 32 : k * 32 + 32] for s in range(4)], axis=1
    )


def select_rows(onehot, values):
    high = values.astype(BF16)
    rest = values - high.astype(F32)
    middle = rest.astype(BF16)
    low = (rest - middle.astype(F32)).astype(BF16)
    width = values.shape[1]
    parts = jnp.concatenate([high, middle, low], axis=1)
    out = jnp.dot(onehot, parts, preferred_element_type=F32)
    return (out[:, :width] + out[:, width : 2 * width]) + out[:, 2 * width :]


def rows_ahead(values, count):
    return pltpu.roll(values, (-count) % 256, 0)


def lanes_ahead(values, count):
    return pltpu.roll(values, (-count) % values.shape[1], 1)


def step_forward(values, direction):
    row = iota(values.shape, 0)
    if direction == 0:
        return rows_ahead(values, 64)
    if direction == 1:
        return jnp.where(row // 16 % 4 == 3, rows_ahead(values, -48), rows_ahead(values, 16))
    return jnp.where(row % 16 == 15, rows_ahead(values, -15), rows_ahead(values, 1))


def step_back(values, direction):
    row = iota(values.shape, 0)
    if direction == 0:
        return rows_ahead(values, -64)
    if direction == 1:
        return jnp.where(row // 16 % 4 == 0, rows_ahead(values, 48), rows_ahead(values, -16))
    return jnp.where(row % 16 == 0, rows_ahead(values, 15), rows_ahead(values, -1))


def partner(values):
    face = iota(values.shape, 1) % 8
    minus = lanes_ahead(values, 3)
    plus = lanes_ahead(values, -3)
    out = step_forward(minus, 0)
    out = jnp.where(face == 1, step_forward(minus, 1), out)
    out = jnp.where(face == 2, step_forward(minus, 2), out)
    out = jnp.where(face == 3, step_back(plus, 0), out)
    out = jnp.where(face == 4, step_back(plus, 1), out)
    return jnp.where(face == 5, step_back(plus, 2), out)


def fetch(sources, targets, sems):
    copies = [
        pltpu.make_async_copy(source, target, sems.at[at])
        for at, (source, target) in enumerate(zip(sources, targets))
    ]
    for copy in copies:
        copy.start()
    return copies


def pack_kernel(
    assign_hbm, corners_hbm, solid_hbm, residual_hbm, stiffness_hbm, out_ref, solid_ref,
    assign, corners, solid, residual, stiffness, sems,
):
    copies = fetch(
        [assign_hbm, corners_hbm, solid_hbm, residual_hbm, stiffness_hbm],
        [assign, corners, solid, residual, stiffness],
        sems,
    )
    for copy in copies:
        copy.wait()
    first = 4 * lax.axis_index("sub")
    res = []
    stiff = []
    ones = jnp.ones((1, 768), F32)
    for s in range(4):
        vertex = jnp.full((1, 768), corners[s, 0].astype(F32), F32)
        place = jnp.full((1, 768), assign[first + s].astype(F32), F32)
        res.append(slot_faces(residual, s, [vertex, place]))
        stiff.append(slot_faces(stiffness, s, [ones, ones]))
    pairs = [((res, 0), (res, 1)), ((res, 2), (stiff, 0)), ((stiff, 1), (stiff, 2))]
    for at, (one, two) in enumerate(pairs):
        a, b = pair_transpose(stack_rows(*one), stack_rows(*two))
        out_ref[:, 0, at * 256 : at * 256 + 128] = a
        out_ref[:, 0, at * 256 + 128 : at * 256 + 256] = b
    pieces = []
    for s in range(4):
        for p in range(4):
            pieces += [solid[s, p : p + 1, :].astype(F32), jnp.zeros((1, 2), F32)]
    solid_ref[...] = jnp.concatenate(pieces, axis=1)


def weigh_kernel(in_ref, out_ref, weight_ref, weight_partner_ref, place_ref, slot_ref, vertex_ref):
    tiles = [in_ref[:, 0, at * 128 : at * 128 + 128] for at in range(6)]
    res = to_slots(tiles[:3])
    stiff = to_slots(tiles[3:])
    lane = iota((256, 256), 1).astype(F32)
    to_place = jnp.where(res[:, 7:8] == lane, 1.0, 0.0).astype(F32)
    from_place = to_place.astype(BF16)
    to_place = to_place.T.astype(BF16)
    both = select_rows(to_place, jnp.concatenate([res, stiff], axis=1))
    res = both[:, :128]
    stiff = both[:, 128:]
    vertex = jnp.broadcast_to(res[:, 6:7], (256, 128)).T[0:1, :]
    entry_vertex = (iota((768, 1), 0) // 3).astype(F32)
    stiff_partner = partner(stiff)
    total = stiff + stiff_partner
    weight = stiff / total
    back = select_rows(from_place, weight * (res + partner(res)))
    for k in range(3):
        out_ref[:, 0, k * 128 : k * 128 + 128] = from_slots(back, k)
    weight_ref[...] = weight
    weight_partner_ref[...] = stiff_partner / total
    place_ref[...] = to_place
    slot_ref[...] = from_place
    vertex_ref[...] = jnp.where(entry_vertex == vertex, 1.0, 0.0).astype(BF16)


def face_mask(shape, index):
    lane = iota(shape, 1)
    return (lane // 32 == index // 6) & (lane % 8 == index % 6)


GROUP = 2
CHUNKS = 24 // GROUP


def solve_kernel(
    in_ref, solid_ref, inverses_hbm, basis_hbm, local_ref, message_ref,
    inverses, basis, rhs, sems,
):
    size = GROUP * 192
    chunks = [pl.ds(at * size, size) for at in range(CHUNKS)]
    copies = fetch(
        [inverses_hbm.at[chunk] for chunk in chunks] + [basis_hbm],
        [inverses.at[chunk] for chunk in chunks] + [basis],
        sems,
    )
    tiles = [in_ref[:, 0, k * 128 : k * 128 + 128] for k in range(3)]
    patch = iota((64, 128), 1) // 8 % 4
    for k in range(3):
        value = tiles[k] * solid_ref[...]
        for p in range(4):
            row = p * 192 + k * 64
            rhs[row : row + 64, :] = jnp.where(patch == p, value, 0.0).astype(BF16)
    held = jnp.zeros((192, 128), F32)
    for chunk in range(CHUNKS):
        copies[chunk].wait()
        product = jnp.dot(
            inverses[chunk * size : chunk * size + size, :], rhs[...], preferred_element_type=F32
        )
        for at in range(GROUP):
            mask = face_mask((192, 128), chunk * GROUP + at)
            held = jnp.where(mask, product[at * 192 : at * 192 + 192], held)
    local_ref[...] = held
    copies[CHUNKS].wait()
    coarse = jnp.dot(basis[...], rhs[...], preferred_element_type=F32)
    parts = []
    for s in range(4):
        part = jnp.zeros((24, 128), F32)
        for f in range(6):
            at = s * 6 + f
            part = part + jnp.where(face_mask((24, 128), at), coarse[at * 24 : at * 24 + 24], 0.0)
        parts += [part, jnp.zeros((8, 128), F32)]
    row = jnp.sum(jnp.concatenate(parts, axis=0).T, axis=0, keepdims=True)
    product_sum = jnp.zeros((64, 128), F32)
    for k in range(3):
        product_sum = product_sum + tiles[k] * held[k * 64 : k * 64 + 64]
    inner = jnp.sum(
        jnp.sum(product_sum, axis=0, keepdims=True) * solid_ref[...], axis=1, keepdims=True
    )
    row = jnp.where(iota((1, 128), 1) == 24, inner, row)
    message_ref[...] = jnp.broadcast_to(row.reshape(1, 1, 128), message_ref.shape)


def coarse_kernel(
    in_ref, place_ref, vertex_ref, local_ref, solid_ref, one_ref, two_ref, three_ref, own_hbm,
    corners_hbm, basis_hbm, out_ref, inner_ref, own_ref, corners_ref, basis_ref, columns, sems,
):
    copies = fetch(
        [own_hbm, corners_hbm, basis_hbm], [own_ref, corners_ref, basis_ref], sems
    )
    summed = in_ref[0:64, 0, :]
    for y in range(1, 4):
        summed = summed + in_ref[y * 64 : y * 64 + 64, 0, :]
    inner = jnp.sum(jnp.sum(summed, axis=0, keepdims=True)[:, 24:25], axis=1, keepdims=True)
    pad = jnp.zeros((64, 96), F32)
    parts = jnp.concatenate(
        [jnp.concatenate([summed[:, s * 32 : s * 32 + 32], pad], axis=1) for s in range(4)], axis=0
    )
    parts = select_rows(place_ref[...], parts)
    for direction, count in ((2, 3), (1, 6), (0, 12)):
        parts = parts + step_back(lanes_ahead(parts, count), direction)
    by_entry = select_rows(vertex_ref[...], parts)
    own = iota((768, 128), 0) % 3 == iota((768, 128), 1)
    column = jnp.sum(jnp.where(own, by_entry, 0.0), axis=1, keepdims=True)
    columns[...] = jnp.broadcast_to(column, (768, 128))
    diagonal = iota((768, 768), 0) == iota((768, 768), 1)
    residual = jnp.sum(jnp.where(diagonal, column, 0.0), axis=0, keepdims=True)
    solution = jnp.zeros((8, 768), F32)
    copies[0].wait()
    for ahead, inverse in enumerate((own_ref, one_ref, two_ref, three_ref)):
        block = lax.rem(lax.axis_index("crs") + ahead, 4) * 192
        factor = columns[pl.ds(pl.multiple_of(block, 8), 192), :]
        pieces = []
        for at in range(6):
            terms = inverse[:, at * 128 : at * 128 + 128] * factor
            pieces.append(jnp.sum(terms.reshape(24, 8, 128), axis=0))
        solution = solution + jnp.concatenate(pieces, axis=1)
    rounded = jnp.sum(solution, axis=0, keepdims=True).astype(BF16).astype(F32)
    inner_ref[...] = inner + jnp.sum(rounded * residual, axis=1, keepdims=True)
    entry = iota((24, 768), 0)
    lane = iota((24, 768), 1)
    copies[1].wait()
    copies[2].wait()
    faces = []
    for s in range(4):
        index = entry % 3
        for c in range(8):
            index = jnp.where(entry // 3 == c, entry % 3 + 3 * corners_ref[s, c], index)
        values = jnp.sum(jnp.where(lane == index, rounded, 0.0), axis=1, keepdims=True)
        rows = []
        for f in range(6):
            block = basis_ref[(s * 6 + f) * 24 : (s * 6 + f) * 24 + 24, :].astype(F32)
            rows.append(jnp.sum(block * values, axis=0, keepdims=True))
        faces.append(jnp.concatenate(rows + [jnp.zeros((2, 768), F32)], axis=0))
    a, b = pair_transpose(stack_rows(faces, 0), stack_rows(faces, 1))
    c, _ = pair_transpose(stack_rows(faces, 2), jnp.zeros((128, 64), F32))
    for k, tile in enumerate((a, b, c)):
        out_ref[:, 0, k * 128 : k * 128 + 128] = solid_ref[...] * (
            local_ref[k * 64 : k * 64 + 64] + tile
        )


def average_kernel(in_ref, place_ref, slot_ref, weight_ref, weight_partner_ref, out_ref):
    tiles = [in_ref[:, 0, k * 128 : k * 128 + 128] for k in range(3)]
    values = select_rows(place_ref[...], to_slots(tiles))
    values = weight_ref[...] * values + weight_partner_ref[...] * partner(values)
    back = select_rows(slot_ref[...], values)
    for k in range(3):
        out_ref[:, 0, k * 128 : k * 128 + 128] = from_slots(back, k)


def unpack_kernel(in_ref, out_ref):
    faces = unpack_faces([in_ref[:, 0, k * 128 : k * 128 + 128] for k in range(3)])
    for f in range(6):
        out_ref[f] = jnp.concatenate([faces[s][f : f + 1, :] for s in range(4)], axis=0)


def spec(space=VMEM):
    return pl.BlockSpec(memory_space=space)


def shaped(*shape, dtype=F32):
    return jax.ShapeDtypeStruct(shape, dtype)


def call(kernel, inputs, outputs, name, scratch=(), megabytes=8):
    run = pl.pallas_call(
        kernel,
        in_specs=[spec(space) for space in inputs],
        out_specs=tuple(spec() for _ in outputs),
        out_shape=tuple(outputs),
        scratch_shapes=scratch,
        name=name,
        compiler_params=pltpu.CompilerParams(vmem_limit_bytes=megabytes * 2**20),
    )

    def placed(*values):
        return run(
            *(
                pltpu.with_memory_space_constraint(value, space) if space is HBM else value
                for value, space in zip(values, inputs)
            )
        )

    return placed


def exchange(values, axes):
    return lax.all_to_all(values, axes, 0, 0)


def body(residual, stiffness, solid, inverses, coarse_basis, assign, corners, coarse_inverse):
    others = [
        lax.ppermute(coarse_inverse, "crs", [(y, (y - ahead) % 4) for y in range(4)])
        for ahead in (1, 2, 3)
    ]
    basis_rows = coarse_basis.transpose(0, 2, 1, 3).reshape(576, 768)
    dma = pltpu.SemaphoreType.DMA

    packed, solid_row = call(
        pack_kernel,
        [HBM] * 5,
        [shaped(64, 1, 768), shaped(1, 128)],
        "pack",
        [
            SMEM((256,), jnp.int32),
            SMEM((4, 8), jnp.int32),
            VMEM((4, 4, 6), jnp.int32),
            VMEM((6, 4, 768), F32),
            VMEM((6, 4, 768), F32),
            dma((5,)),
        ],
    )(
        assign,
        corners,
        solid.transpose(0, 2, 1),
        residual.transpose(1, 0, 2),
        stiffness.transpose(1, 0, 2),
    )
    weighed, weight, weight_partner, to_place, from_place, to_vertex = call(
        weigh_kernel,
        [VMEM],
        [shaped(64, 1, 384), shaped(256, 128), shaped(256, 128)]
        + [shaped(n, 256, dtype=BF16) for n in (256, 256, 768)],
        "weigh",
    )(exchange(packed, "sub"))
    local, message = call(
        solve_kernel,
        [VMEM, VMEM, HBM, HBM],
        [shaped(192, 128), shaped(256, 1, 128)],
        "solve",
        [
            VMEM((4608, 768), BF16),
            VMEM((576, 768), BF16),
            VMEM((768, 128), BF16),
            dma((CHUNKS + 1,)),
        ],
        16,
    )(exchange(weighed, "sub"), solid_row, inverses.reshape(4608, 768), basis_rows)
    solved, inner = call(
        coarse_kernel,
        [VMEM] * 8 + [HBM] * 3,
        [shaped(64, 1, 384), shaped(1, 1)],
        "coarse",
        [
            VMEM((192, 768), F32),
            SMEM((4, 8), jnp.int32),
            VMEM((576, 768), BF16),
            VMEM((768, 128), F32),
            dma((3,)),
        ],
    )(
        exchange(message, ("crs", "sub")),
        to_place,
        to_vertex,
        local,
        solid_row,
        *others,
        coarse_inverse,
        corners,
        basis_rows,
    )
    (averaged,) = call(average_kernel, [VMEM] * 5, [shaped(64, 1, 384)], "average")(
        exchange(solved, "sub"), to_place, from_place, weight, weight_partner
    )
    (out,) = call(unpack_kernel, [VMEM], [shaped(6, 4, 768)], "unpack")(exchange(averaged, "sub"))
    return out.transpose(1, 0, 2), inner.reshape(1)


def solution(mesh):
    return jax.shard_map(
        body,
        mesh=mesh,
        in_specs=(
            P("sub", None, "crs"),
            P("sub", None, "crs"),
            P("sub", None, "crs"),
            P("sub", None, None, "crs"),
            P("sub", None, None, "crs"),
            P(),
            P("sub", None),
            P("crs", None),
        ),
        out_specs=(P("sub", None, "crs"), P()),
        check_vma=False,
    )
```

```python
import jax
import jax.numpy as jnp
from jax import lax
from jax.experimental import pallas as pl
from jax.experimental.pallas import tpu as pltpu
from jax.sharding import PartitionSpec as P


F32 = jnp.float32
BF16 = jnp.bfloat16
VMEM = pltpu.VMEM
SMEM = pltpu.SMEM
HBM = pltpu.HBM


def iota(shape, axis):
    return lax.broadcasted_iota(jnp.int32, shape, axis)


def pair_transpose(first, second):
    both = jnp.concatenate([first, second], axis=1)
    turned = both.T
    return turned[:64], turned[64:]


def stack_rows(faces, k):
    return jnp.concatenate(
        [
            faces[s][:, p * 192 + k * 64 : p * 192 + k * 64 + 64]
            for s in range(4)
            for p in range(4)
        ],
        axis=0,
    )


def slot_faces(ref, s, pads):
    return jnp.concatenate([ref[f, s : s + 1, :] for f in range(6)] + pads, axis=0)


def unpack_faces(tiles):
    first = jnp.concatenate([tiles[0], tiles[1]], axis=0).T
    second = jnp.concatenate([tiles[2], jnp.zeros_like(tiles[2])], axis=0).T
    faces = []
    for s in range(4):
        pieces = []
        for p in range(4):
            row = s * 32 + p * 8
            pieces += [first[row : row + 8], second[row : row + 8, :64]]
        faces.append(jnp.concatenate(pieces, axis=1))
    return faces


def to_slots(tiles):
    pad = jnp.zeros((64, 32), F32)
    return jnp.concatenate(
        [
            jnp.concatenate([tile[:, s * 32 : s * 32 + 32] for tile in tiles] + [pad], axis=1)
            for s in range(4)
        ],
        axis=0,
    )


def from_slots(rows, k):
    return jnp.concatenate(
        [rows[s * 64 : s * 64 + 64, k * 32 : k * 32 + 32] for s in range(4)], axis=1
    )


def split(values):
    high = values.astype(BF16)
    rest = values - high.astype(F32)
    middle = rest.astype(BF16)
    return high, middle, (rest - middle.astype(F32)).astype(BF16)


def select_rows(onehot, values):
    width = values.shape[1]
    out = jnp.dot(
        onehot, jnp.concatenate(split(values), axis=1), preferred_element_type=F32
    )
    return (out[:, :width] + out[:, width : 2 * width]) + out[:, 2 * width :]


def rows_ahead(values, count):
    return pltpu.roll(values, (-count) % 256, 0)


def lanes_ahead(values, count):
    return pltpu.roll(values, (-count) % values.shape[1], 1)


def step_forward(values, direction):
    row = iota(values.shape, 0)
    if direction == 0:
        return rows_ahead(values, 64)
    if direction == 1:
        return jnp.where(row // 16 % 4 == 3, rows_ahead(values, -48), rows_ahead(values, 16))
    return jnp.where(row % 16 == 15, rows_ahead(values, -15), rows_ahead(values, 1))


def step_back(values, direction):
    row = iota(values.shape, 0)
    if direction == 0:
        return rows_ahead(values, -64)
    if direction == 1:
        return jnp.where(row // 16 % 4 == 0, rows_ahead(values, 48), rows_ahead(values, -16))
    return jnp.where(row % 16 == 0, rows_ahead(values, 15), rows_ahead(values, -1))


def partner(values):
    face = iota(values.shape, 1) % 8
    minus = lanes_ahead(values, 3)
    plus = lanes_ahead(values, -3)
    out = step_forward(minus, 0)
    out = jnp.where(face == 1, step_forward(minus, 1), out)
    out = jnp.where(face == 2, step_forward(minus, 2), out)
    out = jnp.where(face == 3, step_back(plus, 0), out)
    out = jnp.where(face == 4, step_back(plus, 1), out)
    return jnp.where(face == 5, step_back(plus, 2), out)


def fetch(sources, targets, sems):
    copies = [
        pltpu.make_async_copy(source, target, sems.at[at])
        for at, (source, target) in enumerate(zip(sources, targets))
    ]
    for copy in copies:
        copy.start()
    return copies


def pack_kernel(
    assign_hbm, corners_hbm, solid_hbm, residual_hbm, stiffness_hbm, out_ref, solid_ref,
    assign, corners, solid, residual, stiffness, sems,
):
    copies = fetch(
        [assign_hbm, corners_hbm, solid_hbm, residual_hbm, stiffness_hbm],
        [assign, corners, solid, residual, stiffness],
        sems,
    )
    for copy in copies:
        copy.wait()
    first = 4 * lax.axis_index("sub")
    res = []
    stiff = []
    ones = jnp.ones((1, 768), F32)
    for s in range(4):
        vertex = jnp.full((1, 768), corners[s, 0].astype(F32), F32)
        place = jnp.full((1, 768), assign[first + s].astype(F32), F32)
        res.append(slot_faces(residual, s, [vertex, place]))
        stiff.append(slot_faces(stiffness, s, [ones, ones]))
    pairs = [((res, 0), (res, 1)), ((res, 2), (stiff, 0)), ((stiff, 1), (stiff, 2))]
    for at, (one, two) in enumerate(pairs):
        a, b = pair_transpose(stack_rows(*one), stack_rows(*two))
        out_ref[:, 0, at * 256 : at * 256 + 128] = a
        out_ref[:, 0, at * 256 + 128 : at * 256 + 256] = b
    pieces = []
    for s in range(4):
        for p in range(4):
            pieces += [solid[s, p : p + 1, :].astype(F32), jnp.zeros((1, 2), F32)]
    solid_ref[...] = jnp.concatenate(pieces, axis=1)


def weigh_kernel(in_ref, out_ref, weight_ref, weight_partner_ref, place_ref, slot_ref, vertex_ref):
    tiles = [in_ref[:, 0, at * 128 : at * 128 + 128] for at in range(6)]
    res = to_slots(tiles[:3])
    stiff = to_slots(tiles[3:])
    lane = iota((256, 256), 1).astype(F32)
    to_place = jnp.where(res[:, 7:8] == lane, 1.0, 0.0).astype(F32)
    from_place = to_place.astype(BF16)
    to_place = to_place.T.astype(BF16)
    both = select_rows(to_place, jnp.concatenate([res, stiff], axis=1))
    res = both[:, :128]
    stiff = both[:, 128:]
    stiff_partner = partner(stiff)
    total = stiff + stiff_partner
    weight = stiff / total
    back = select_rows(from_place, weight * (res + partner(res)))
    for k in range(3):
        out_ref[:, 0, k * 128 : k * 128 + 128] = from_slots(back, k)
    weight_ref[...] = weight
    weight_partner_ref[...] = stiff_partner / total
    place_ref[...] = to_place
    slot_ref[...] = from_place
    vertex_ref[...] = res


def face_mask(shape, index):
    lane = iota(shape, 1)
    return (lane // 32 == index // 6) & (lane % 8 == index % 6)


STEPS = 2


def solve_kernel(
    in_ref, solid_ref, inverses, basis_hbm, local_ref, message_ref, basis, rhs, total, sem
):
    step = pl.program_id(0)
    faces = 24 // STEPS
    copy = pltpu.make_async_copy(basis_hbm, basis, sem)

    @pl.when(step == 0)
    def _():
        copy.start()
        patch = iota((64, 128), 1) // 8 % 4
        for k in range(3):
            value = in_ref[:, 0, k * 128 : k * 128 + 128] * solid_ref[...]
            for p in range(4):
                row = p * 192 + k * 64
                rhs[row : row + 64, :] = jnp.where(patch == p, value, 0.0).astype(BF16)
        total[...] = jnp.zeros_like(total)

    product = jnp.dot(inverses[...], rhs[...], preferred_element_type=F32)
    held = total[...]
    for at in range(faces):
        mask = face_mask((192, 128), step * faces + at)
        held = jnp.where(mask, product[at * 192 : at * 192 + 192], held)
    total[...] = held

    @pl.when(step == STEPS - 1)
    def _():
        copy.wait()
        coarse = jnp.dot(basis[...], rhs[...], preferred_element_type=F32)
        parts = []
        for s in range(4):
            part = jnp.zeros((24, 128), F32)
            for f in range(6):
                at = s * 6 + f
                part = part + jnp.where(
                    face_mask((24, 128), at), coarse[at * 24 : at * 24 + 24], 0.0
                )
            parts += [part, jnp.zeros((8, 128), F32)]
        row = jnp.sum(jnp.concatenate(parts, axis=0).T, axis=0, keepdims=True)
        product_sum = jnp.zeros((64, 128), F32)
        for k in range(3):
            product_sum = product_sum + in_ref[:, 0, k * 128 : k * 128 + 128] * (
                held[k * 64 : k * 64 + 64]
            )
        inner = jnp.sum(
            jnp.sum(product_sum, axis=0, keepdims=True) * solid_ref[...], axis=1, keepdims=True
        )
        row = jnp.where(iota((1, 128), 1) == 24, inner, row)
        message_ref[...] = jnp.broadcast_to(row.reshape(1, 1, 128), message_ref.shape)
        local_ref[...] = held


def pick_kernel(
    after_ref, vertex_ref, one_ref, two_ref, three_ref, own_hbm, corners_hbm, out_ref, own_ref,
    corners_ref, columns, sems,
):
    copies = fetch([own_hbm, corners_hbm], [own_ref, corners_ref], sems)
    lane = iota((1, 128), 1)
    index = jnp.full((1, 128), -1, jnp.int32)
    copies[1].wait()
    for s in range(4):
        for c in range(8):
            first = s * 32 + c * 3
            here = (lane >= first) & (lane < first + 3)
            index = jnp.where(here, 3 * corners_ref[s, c] + lane - first, index)
    wanted = jnp.where(iota((768, 128), 0) == index, 1.0, 0.0).astype(BF16)
    copies[0].wait()
    for ahead, inverse in enumerate((own_ref, one_ref, two_ref, three_ref)):
        block = lax.rem(lax.axis_index("crs") + ahead, 4) * 192
        picked = jnp.dot(
            jnp.concatenate(split(inverse[...]), axis=0), wanted, preferred_element_type=F32
        )
        columns[pl.ds(pl.multiple_of(block, 8), 192), :] = (
            picked[:192] + picked[192:384]
        ) + picked[384:]
    vertex = 3.0 * vertex_ref[:, 6:7]
    entry = iota((256, 768), 1).astype(F32)
    values = columns[...]
    for j in range(3):
        rows = jnp.where(entry == vertex + j, 1.0, 0.0).astype(BF16)
        out_ref[j * 256 : j * 256 + 256, :] = select_rows(rows, values)


def coarse_kernel(
    in_ref, place_ref, picked_ref, local_ref, solid_ref, basis_hbm, out_ref, basis_ref, sem
):
    copy = pltpu.make_async_copy(basis_hbm, basis_ref, sem)
    copy.start()
    summed = in_ref[0:64, 0, :]
    me = lax.axis_index("sub")
    mine = in_ref[pl.ds(me, 1), 0, :]
    for y in range(1, 4):
        summed = summed + in_ref[y * 64 : y * 64 + 64, 0, :]
        mine = mine + in_ref[pl.ds(y * 64 + me, 1), 0, :]
    parts = jnp.concatenate([summed[:, s * 32 : s * 32 + 32] for s in range(4)], axis=0)
    parts = jnp.concatenate(
        [part.astype(F32) for part in split(parts)] + [jnp.zeros((256, 32), F32)], axis=1
    )
    parts = jnp.dot(place_ref[...], parts.astype(BF16), preferred_element_type=F32)
    parts = (parts + lanes_ahead(parts, 32)) + lanes_ahead(parts, 64)
    for direction, count in ((2, 3), (1, 6), (0, 12)):
        parts = parts + step_back(lanes_ahead(parts, count), direction)
    terms = jnp.zeros((256, 128), F32)
    for j in range(3):
        terms = terms + picked_ref[j * 256 : j * 256 + 256, :] * parts[:, j : j + 1]
    rounded = jnp.sum(terms, axis=0, keepdims=True).astype(BF16).astype(F32)
    inner = jnp.sum(rounded * mine, axis=1, keepdims=True) + mine[:, 24:25]
    values = jnp.broadcast_to(rounded, (128, 128)).T
    copy.wait()
    faces = []
    for s in range(4):
        rows = []
        for f in range(6):
            at = s * 6 + f
            block = basis_ref[at * 24 : at * 24 + 24, :].astype(F32)
            factor = values[s * 32 : s * 32 + 24, 0:1]
            rows.append(jnp.sum(block * factor, axis=0, keepdims=True))
        faces.append(jnp.concatenate(rows + [jnp.zeros((2, 768), F32)], axis=0))
    a, b = pair_transpose(stack_rows(faces, 0), stack_rows(faces, 1))
    c, _ = pair_transpose(stack_rows(faces, 2), jnp.zeros((128, 64), F32))
    for k, tile in enumerate((a, b, c)):
        tile = solid_ref[...] * (local_ref[k * 64 : k * 64 + 64] + tile)
        if k == 0:
            tile = jnp.where(iota((64, 128), 1) == 6, inner, tile)
        out_ref[:, 0, k * 128 : k * 128 + 128] = tile


def average_kernel(in_ref, place_ref, slot_ref, weight_ref, weight_partner_ref, out_ref):
    tiles = [in_ref[:, 0, k * 128 : k * 128 + 128] for k in range(3)]
    inner = jnp.sum(tiles[0], axis=0, keepdims=True)[:, 6:7]
    values = select_rows(place_ref[...], to_slots(tiles))
    values = weight_ref[...] * values + weight_partner_ref[...] * partner(values)
    back = select_rows(slot_ref[...], values)
    for k in range(3):
        tile = from_slots(back, k)
        if k == 0:
            tile = jnp.where(iota((64, 128), 1) == 6, inner, tile)
        out_ref[:, 0, k * 128 : k * 128 + 128] = tile


def unpack_kernel(in_ref, out_ref, inner_ref):
    inner_ref[...] = in_ref[0:1, 0, 6:7]
    faces = unpack_faces([in_ref[:, 0, k * 128 : k * 128 + 128] for k in range(3)])
    for f in range(6):
        out_ref[f] = jnp.concatenate([faces[s][f : f + 1, :] for s in range(4)], axis=0)


def spec(space=VMEM):
    return pl.BlockSpec(memory_space=space)


def shaped(*shape, dtype=F32):
    return jax.ShapeDtypeStruct(shape, dtype)


def call(kernel, inputs, outputs, name, scratch=(), megabytes=8):
    run = pl.pallas_call(
        kernel,
        in_specs=[spec(space) for space in inputs],
        out_specs=tuple(spec() for _ in outputs),
        out_shape=tuple(outputs),
        scratch_shapes=scratch,
        name=name,
        compiler_params=pltpu.CompilerParams(vmem_limit_bytes=megabytes * 2**20),
    )

    def placed(*values):
        return run(
            *(
                pltpu.with_memory_space_constraint(value, space) if space is HBM else value
                for value, space in zip(values, inputs)
            )
        )

    return placed


def exchange(values, axes):
    return lax.all_to_all(values, axes, 0, 0)


def body(residual, stiffness, solid, inverses, coarse_basis, assign, corners, coarse_inverse):
    others = [
        lax.ppermute(coarse_inverse, "crs", [(y, (y - ahead) % 4) for y in range(4)])
        for ahead in (1, 2, 3)
    ]
    basis_rows = coarse_basis.transpose(0, 2, 1, 3).reshape(576, 768)
    dma = pltpu.SemaphoreType.DMA

    packed, solid_row = call(
        pack_kernel,
        [HBM] * 5,
        [shaped(64, 1, 768), shaped(1, 128)],
        "pack",
        [
            SMEM((256,), jnp.int32),
            SMEM((4, 8), jnp.int32),
            VMEM((4, 4, 6), jnp.int32),
            VMEM((6, 4, 768), F32),
            VMEM((6, 4, 768), F32),
            dma((5,)),
        ],
    )(
        assign,
        corners,
        solid.transpose(0, 2, 1),
        residual.transpose(1, 0, 2),
        stiffness.transpose(1, 0, 2),
    )
    weighed, weight, weight_partner, to_place, from_place, vertex = call(
        weigh_kernel,
        [VMEM],
        [
            shaped(64, 1, 384),
            shaped(256, 128),
            shaped(256, 128),
            shaped(256, 256, dtype=BF16),
            shaped(256, 256, dtype=BF16),
            shaped(256, 128),
        ],
        "weigh",
    )(exchange(packed, "sub"))
    whole = [pl.BlockSpec(memory_space=VMEM), pl.BlockSpec(memory_space=HBM)]
    rows = 4608 // STEPS
    local, message = pl.pallas_call(
        solve_kernel,
        grid=(STEPS,),
        in_specs=[whole[0], whole[0], pl.BlockSpec((rows, 768), lambda i: (i, 0)), whole[1]],
        out_specs=(whole[0], whole[0]),
        out_shape=(shaped(192, 128), shaped(256, 1, 128)),
        scratch_shapes=[
            VMEM((576, 768), BF16),
            VMEM((768, 128), BF16),
            VMEM((192, 128), F32),
            dma(()),
        ],
        name="solve",
        compiler_params=pltpu.CompilerParams(vmem_limit_bytes=16 * 2**20),
    )(
        exchange(weighed, "sub"),
        solid_row,
        pltpu.with_memory_space_constraint(inverses.reshape(4608, 768), HBM),
        pltpu.with_memory_space_constraint(basis_rows, HBM),
    )
    (picked,) = call(
        pick_kernel,
        [VMEM] * 5 + [HBM] * 2,
        [shaped(768, 128)],
        "pick",
        [
            VMEM((192, 768), F32),
            SMEM((4, 8), jnp.int32),
            VMEM((768, 128), F32),
            dma((2,)),
        ],
    )(local, vertex, *others, coarse_inverse, corners)
    (solved,) = call(
        coarse_kernel,
        [VMEM] * 5 + [HBM],
        [shaped(64, 1, 384)],
        "coarse",
        [VMEM((576, 768), BF16), dma(())],
    )(exchange(message, ("crs", "sub")), to_place, picked, local, solid_row, basis_rows)
    (averaged,) = call(average_kernel, [VMEM] * 5, [shaped(64, 1, 384)], "average")(
        exchange(solved, "sub"), to_place, from_place, weight, weight_partner
    )
    out, inner = call(unpack_kernel, [VMEM], [shaped(6, 4, 768), shaped(1, 1)], "unpack")(
        exchange(averaged, "sub")
    )
    return out.transpose(1, 0, 2), inner.reshape(1)


def solution(mesh):
    return jax.shard_map(
        body,
        mesh=mesh,
        in_specs=(
            P("sub", None, "crs"),
            P("sub", None, "crs"),
            P("sub", None, "crs"),
            P("sub", None, None, "crs"),
            P("sub", None, None, "crs"),
            P(),
            P("sub", None),
            P("crs", None),
        ),
        out_specs=(P("sub", None, "crs"), P()),
        check_vma=False,
    )
```

```python
import jax
import jax.numpy as jnp
from jax import lax
from jax.experimental import pallas as pl
from jax.experimental.pallas import tpu as pltpu
from jax.sharding import PartitionSpec as P


F32 = jnp.float32
BF16 = jnp.bfloat16
VMEM = pltpu.VMEM
SMEM = pltpu.SMEM
HBM = pltpu.HBM


def iota(shape, axis):
    return lax.broadcasted_iota(jnp.int32, shape, axis)


def pair_transpose(first, second):
    both = jnp.concatenate([first, second], axis=1)
    turned = both.T
    return turned[:64], turned[64:]


def stack_rows(faces, k):
    return jnp.concatenate(
        [
            faces[s][:, p * 192 + k * 64 : p * 192 + k * 64 + 64]
            for s in range(4)
            for p in range(4)
        ],
        axis=0,
    )


def slot_faces(ref, s, pads):
    return jnp.concatenate([ref[f, s : s + 1, :] for f in range(6)] + pads, axis=0)


def unpack_faces(tiles):
    first = jnp.concatenate([tiles[0], tiles[1]], axis=0).T
    second = jnp.concatenate([tiles[2], jnp.zeros_like(tiles[2])], axis=0).T
    faces = []
    for s in range(4):
        pieces = []
        for p in range(4):
            row = s * 32 + p * 8
            pieces += [first[row : row + 8], second[row : row + 8, :64]]
        faces.append(jnp.concatenate(pieces, axis=1))
    return faces


def to_slots(tiles):
    pad = jnp.zeros((64, 32), F32)
    return jnp.concatenate(
        [
            jnp.concatenate([tile[:, s * 32 : s * 32 + 32] for tile in tiles] + [pad], axis=1)
            for s in range(4)
        ],
        axis=0,
    )


def from_slots(rows, k):
    return jnp.concatenate(
        [rows[s * 64 : s * 64 + 64, k * 32 : k * 32 + 32] for s in range(4)], axis=1
    )


def split(values):
    high = values.astype(BF16)
    rest = values - high.astype(F32)
    middle = rest.astype(BF16)
    return high, middle, (rest - middle.astype(F32)).astype(BF16)


def select_rows(onehot, values):
    width = values.shape[1]
    out = jnp.dot(
        onehot, jnp.concatenate(split(values), axis=1), preferred_element_type=F32
    )
    return (out[:, :width] + out[:, width : 2 * width]) + out[:, 2 * width :]


def rows_ahead(values, count):
    return pltpu.roll(values, (-count) % 256, 0)


def lanes_ahead(values, count):
    return pltpu.roll(values, (-count) % values.shape[1], 1)


def step_forward(values, direction):
    row = iota(values.shape, 0)
    if direction == 0:
        return rows_ahead(values, 64)
    if direction == 1:
        return jnp.where(row // 16 % 4 == 3, rows_ahead(values, -48), rows_ahead(values, 16))
    return jnp.where(row % 16 == 15, rows_ahead(values, -15), rows_ahead(values, 1))


def step_back(values, direction):
    row = iota(values.shape, 0)
    if direction == 0:
        return rows_ahead(values, -64)
    if direction == 1:
        return jnp.where(row // 16 % 4 == 0, rows_ahead(values, 48), rows_ahead(values, -16))
    return jnp.where(row % 16 == 0, rows_ahead(values, 15), rows_ahead(values, -1))


def partner(values):
    face = iota(values.shape, 1) % 8
    minus = lanes_ahead(values, 3)
    plus = lanes_ahead(values, -3)
    out = step_forward(minus, 0)
    out = jnp.where(face == 1, step_forward(minus, 1), out)
    out = jnp.where(face == 2, step_forward(minus, 2), out)
    out = jnp.where(face == 3, step_back(plus, 0), out)
    out = jnp.where(face == 4, step_back(plus, 1), out)
    return jnp.where(face == 5, step_back(plus, 2), out)


def fetch(sources, targets, sems):
    copies = [
        pltpu.make_async_copy(source, target, sems.at[at])
        for at, (source, target) in enumerate(zip(sources, targets))
    ]
    for copy in copies:
        copy.start()
    return copies


def pack_kernel(
    assign_hbm, corners_hbm, solid_hbm, residual_hbm, stiffness_hbm, out_ref, solid_ref,
    assign, corners, solid, residual, stiffness, sems,
):
    copies = fetch(
        [assign_hbm, corners_hbm, solid_hbm, residual_hbm, stiffness_hbm],
        [assign, corners, solid, residual, stiffness],
        sems,
    )
    for copy in copies:
        copy.wait()
    first = 4 * lax.axis_index("sub")
    res = []
    stiff = []
    ones = jnp.ones((1, 768), F32)
    for s in range(4):
        vertex = jnp.full((1, 768), corners[s, 0].astype(F32), F32)
        place = jnp.full((1, 768), assign[first + s].astype(F32), F32)
        res.append(slot_faces(residual, s, [vertex, place]))
        stiff.append(slot_faces(stiffness, s, [ones, ones]))
    pairs = [((res, 0), (res, 1)), ((res, 2), (stiff, 0)), ((stiff, 1), (stiff, 2))]
    for at, (one, two) in enumerate(pairs):
        a, b = pair_transpose(stack_rows(*one), stack_rows(*two))
        out_ref[:, 0, at * 256 : at * 256 + 128] = a
        out_ref[:, 0, at * 256 + 128 : at * 256 + 256] = b
    pieces = []
    for s in range(4):
        for p in range(4):
            pieces += [solid[s, p : p + 1, :].astype(F32), jnp.zeros((1, 2), F32)]
    solid_ref[...] = jnp.concatenate(pieces, axis=1)


def weigh_kernel(in_ref, out_ref, weight_ref, place_ref, slot_ref, vertex_ref):
    tiles = [in_ref[:, 0, at * 128 : at * 128 + 128] for at in range(6)]
    res = to_slots(tiles[:3])
    stiff = to_slots(tiles[3:])
    lane = iota((256, 256), 1).astype(F32)
    to_place = jnp.where(res[:, 7:8] == lane, 1.0, 0.0).astype(F32)
    from_place = to_place.astype(BF16)
    to_place = to_place.T.astype(BF16)
    both = select_rows(to_place, jnp.concatenate([res, stiff], axis=1))
    res = both[:, :128]
    stiff = both[:, 128:]
    weight = stiff / (stiff + partner(stiff))
    back = select_rows(from_place, weight * (res + partner(res)))
    for k in range(3):
        out_ref[:, 0, k * 128 : k * 128 + 128] = from_slots(back, k)
    weight_ref[...] = weight
    place_ref[...] = to_place
    slot_ref[...] = from_place
    vertex_ref[...] = jnp.broadcast_to(res[:, 6:7], (256, 128)).T[0:1]


def face_mask(shape, index):
    lane = iota(shape, 1)
    return (lane // 32 == index // 6) & (lane % 8 == index % 6)


def parts_kernel(in_ref, solid_ref, basis, message_ref, rhs):
    patch = iota((64, 128), 1) // 8 % 4
    for k in range(3):
        value = in_ref[:, 0, k * 128 : k * 128 + 128] * solid_ref[...]
        for p in range(4):
            row = p * 192 + k * 64
            rhs[row : row + 64, :] = jnp.where(patch == p, value, 0.0).astype(BF16)
    coarse = jnp.dot(basis[...], rhs[...], preferred_element_type=F32)
    parts = []
    for s in range(4):
        part = jnp.zeros((24, 128), F32)
        for f in range(6):
            at = s * 6 + f
            part = part + jnp.where(face_mask((24, 128), at), coarse[at * 24 : at * 24 + 24], 0.0)
        parts += [part, jnp.zeros((8, 128), F32)]
    row = jnp.sum(jnp.concatenate(parts, axis=0).T, axis=0, keepdims=True)
    message_ref[...] = jnp.broadcast_to(row.reshape(1, 1, 128), message_ref.shape)


STEPS = 2


def solve_kernel(in_ref, solid_ref, rhs, inverses, local_ref, inner_ref):
    step = pl.program_id(0)
    faces = 24 // STEPS

    @pl.when(step == 0)
    def _():
        local_ref[...] = jnp.zeros_like(local_ref)

    product = jnp.dot(inverses[...], rhs[...], preferred_element_type=F32)
    held = local_ref[...]
    for at in range(faces):
        mask = face_mask((192, 128), step * faces + at)
        held = jnp.where(mask, product[at * 192 : at * 192 + 192], held)
    local_ref[...] = held

    @pl.when(step == STEPS - 1)
    def _():
        product_sum = jnp.zeros((64, 128), F32)
        for k in range(3):
            product_sum = product_sum + in_ref[:, 0, k * 128 : k * 128 + 128] * (
                held[k * 64 : k * 64 + 64]
            )
        inner = jnp.sum(
            jnp.sum(product_sum, axis=0, keepdims=True) * solid_ref[...], axis=1, keepdims=True
        )
        inner_ref[...] = jnp.broadcast_to(inner, (1, 128))


def columns_kernel(
    after_ref, inverse_hbm, corners_hbm, basis_hbm, out_ref, basis_ref, inverse, corners, sems
):
    copies = fetch(
        [inverse_hbm, corners_hbm, basis_hbm], [inverse, corners, basis_ref], sems
    )
    lane = iota((1, 128), 1)
    index = jnp.full((1, 128), -1, jnp.int32)
    copies[1].wait()
    for s in range(4):
        for c in range(8):
            first = s * 32 + c * 3
            here = (lane >= first) & (lane < first + 3)
            index = jnp.where(here, 3 * corners[s, c] + lane - first, index)
    wanted = jnp.where(iota((768, 128), 0) == index, 1.0, 0.0).astype(BF16)
    copies[0].wait()
    picked = jnp.dot(
        jnp.concatenate(split(inverse[...]), axis=0), wanted, preferred_element_type=F32
    )
    out_ref[...] = jnp.concatenate([picked[:192], picked[192:384], picked[384:]], axis=1)
    copies[2].wait()


def pick_kernel(after_ref, vertex_ref, own_ref, one_ref, two_ref, three_ref, out_ref, columns):
    for ahead, block_ref in enumerate((own_ref, one_ref, two_ref, three_ref)):
        block = lax.rem(lax.axis_index("crs") + ahead, 4) * 192
        columns[pl.ds(pl.multiple_of(block, 8), 192), :] = block_ref[...]
    parts = columns[...].astype(BF16)
    vertex = 3.0 * jnp.broadcast_to(vertex_ref[...], (128, 256)).T[:, 0:1]
    entry = iota((256, 768), 1).astype(F32)
    for j in range(3):
        rows = jnp.where(entry == vertex + j, 1.0, 0.0).astype(BF16)
        out = jnp.dot(rows, parts, preferred_element_type=F32)
        out_ref[j * 256 : j * 256 + 256, :] = (out[:, :128] + out[:, 128:256]) + out[:, 256:]


def coarse_kernel(
    in_ref, place_ref, picked_ref, local_ref, inner_ref, near_ref, solid_ref, basis_ref, out_ref
):
    summed = in_ref[0:64, 0, :]
    me = lax.axis_index("sub")
    mine = in_ref[pl.ds(me, 1), 0, :]
    for y in range(1, 4):
        summed = summed + in_ref[y * 64 : y * 64 + 64, 0, :]
        mine = mine + in_ref[pl.ds(y * 64 + me, 1), 0, :]
    parts = jnp.concatenate([summed[:, s * 32 : s * 32 + 32] for s in range(4)], axis=0)
    parts = jnp.concatenate(
        [part.astype(F32) for part in split(parts)] + [jnp.zeros((256, 32), F32)], axis=1
    )
    parts = jnp.dot(place_ref[...], parts.astype(BF16), preferred_element_type=F32)
    parts = (parts + lanes_ahead(parts, 32)) + lanes_ahead(parts, 64)
    for direction, count in ((2, 3), (1, 6), (0, 12)):
        parts = parts + step_back(lanes_ahead(parts, count), direction)
    terms = jnp.zeros((256, 128), F32)
    for j in range(3):
        terms = terms + picked_ref[j * 256 : j * 256 + 256, :] * parts[:, j : j + 1]
    rounded = jnp.sum(terms, axis=0, keepdims=True).astype(BF16).astype(F32)
    inner = jnp.sum(rounded * mine, axis=1, keepdims=True)
    inner = (inner_ref[...] + near_ref[...]) + 0.5 * inner
    values = jnp.broadcast_to(rounded, (128, 128)).T
    faces = []
    for s in range(4):
        rows = []
        for f in range(6):
            at = s * 6 + f
            block = basis_ref[at * 24 : at * 24 + 24, :].astype(F32)
            factor = values[s * 32 : s * 32 + 24, 0:1]
            rows.append(jnp.sum(block * factor, axis=0, keepdims=True))
        faces.append(jnp.concatenate(rows + [jnp.zeros((2, 768), F32)], axis=0))
    a, b = pair_transpose(stack_rows(faces, 0), stack_rows(faces, 1))
    c, _ = pair_transpose(stack_rows(faces, 2), jnp.zeros((128, 64), F32))
    for k, tile in enumerate((a, b, c)):
        tile = solid_ref[...] * (local_ref[k * 64 : k * 64 + 64] + tile)
        if k == 0:
            tile = jnp.where(iota((64, 128), 1) == 6, inner, tile)
        out_ref[:, 0, k * 128 : k * 128 + 128] = tile


def average_kernel(in_ref, place_ref, slot_ref, weight_ref, out_ref, inner_ref):
    tiles = [in_ref[:, 0, k * 128 : k * 128 + 128] for k in range(3)]
    inner_ref[...] = jnp.sum(tiles[0], axis=0, keepdims=True)
    values = select_rows(place_ref[...], to_slots(tiles))
    weight = weight_ref[...]
    values = weight * values + (1.0 - weight) * partner(values)
    back = select_rows(slot_ref[...], values)
    for k in range(3):
        out_ref[:, 0, k * 128 : k * 128 + 128] = from_slots(back, k)


def unpack_kernel(in_ref, sum_ref, far_ref, out_ref, inner_ref):
    inner_ref[...] = (sum_ref[...] + far_ref[...])[:, 6:7]
    faces = unpack_faces([in_ref[:, 0, k * 128 : k * 128 + 128] for k in range(3)])
    for f in range(6):
        out_ref[f] = jnp.concatenate([faces[s][f : f + 1, :] for s in range(4)], axis=0)


def spec(space=VMEM):
    return pl.BlockSpec(memory_space=space)


def shaped(*shape, dtype=F32):
    return jax.ShapeDtypeStruct(shape, dtype)


def call(kernel, inputs, outputs, name, scratch=(), megabytes=8):
    run = pl.pallas_call(
        kernel,
        in_specs=[spec(space) for space in inputs],
        out_specs=tuple(spec() for _ in outputs),
        out_shape=tuple(outputs),
        scratch_shapes=scratch,
        name=name,
        compiler_params=pltpu.CompilerParams(vmem_limit_bytes=megabytes * 2**20),
    )

    def placed(*values):
        return run(
            *(
                pltpu.with_memory_space_constraint(value, space) if space is HBM else value
                for value, space in zip(values, inputs)
            )
        )

    return placed


def exchange(values, axes):
    return lax.all_to_all(values, axes, 0, 0)


def from_ahead(values, ahead):
    return lax.ppermute(values, "crs", [(y, (y - ahead) % 4) for y in range(4)])


def body(residual, stiffness, solid, inverses, coarse_basis, assign, corners, coarse_inverse):
    basis_rows = coarse_basis.transpose(0, 2, 1, 3).reshape(576, 768)
    dma = pltpu.SemaphoreType.DMA

    packed, solid_row = call(
        pack_kernel,
        [HBM] * 5,
        [shaped(64, 1, 768), shaped(1, 128)],
        "pack",
        [
            SMEM((256,), jnp.int32),
            SMEM((4, 8), jnp.int32),
            VMEM((4, 4, 6), jnp.int32),
            VMEM((6, 4, 768), F32),
            VMEM((6, 4, 768), F32),
            dma((5,)),
        ],
    )(
        assign,
        corners,
        solid.transpose(0, 2, 1),
        residual.transpose(1, 0, 2),
        stiffness.transpose(1, 0, 2),
    )
    own_columns, basis_here = call(
        columns_kernel,
        [VMEM, HBM, HBM, HBM],
        [shaped(192, 384), VMEM((576, 768), BF16)],
        "columns",
        [VMEM((192, 768), F32), SMEM((4, 8), jnp.int32), dma((3,))],
    )(solid_row, coarse_inverse, corners, basis_rows)
    arrived, own_columns, basis_here = lax.optimization_barrier(
        (exchange(packed, "sub"), own_columns, basis_here)
    )
    weighed, weight, to_place, from_place, vertex = call(
        weigh_kernel,
        [VMEM],
        [
            shaped(64, 1, 384),
            shaped(256, 128),
            shaped(256, 256, dtype=BF16),
            shaped(256, 256, dtype=BF16),
            shaped(1, 256),
        ],
        "weigh",
    )(arrived)
    others = [from_ahead(own_columns, k) for k in (1, 2, 3)]
    received = exchange(weighed, "sub")
    message, rhs = call(
        parts_kernel,
        [VMEM] * 3,
        [shaped(256, 1, 128), shaped(768, 128, dtype=BF16)],
        "parts",
    )(received, solid_row, basis_here)
    whole = pl.BlockSpec(memory_space=VMEM)
    rows = 4608 // STEPS
    local, inner_part = pl.pallas_call(
        solve_kernel,
        grid=(STEPS,),
        in_specs=[whole, whole, whole, pl.BlockSpec((rows, 768), lambda i: (i, 0))],
        out_specs=(whole, whole),
        out_shape=(shaped(192, 128), shaped(1, 128)),
        name="solve",
        compiler_params=pltpu.CompilerParams(vmem_limit_bytes=16 * 2**20),
    )(
        received,
        solid_row,
        rhs,
        pltpu.with_memory_space_constraint(inverses.reshape(4608, 768), HBM),
    )
    (picked,) = call(
        pick_kernel, [VMEM] * 6, [shaped(768, 128)], "pick", [VMEM((768, 384), F32)]
    )(rhs, vertex, own_columns, *others)
    inner_near = lax.ppermute(inner_part, "crs", [(y, y ^ 1) for y in range(4)])
    (solved,) = call(coarse_kernel, [VMEM] * 8, [shaped(64, 1, 384)], "coarse")(
        exchange(message, ("crs", "sub")),
        to_place,
        picked,
        local,
        inner_part,
        inner_near,
        solid_row,
        basis_here,
    )
    averaged, inner_sum = call(
        average_kernel, [VMEM] * 4, [shaped(64, 1, 384), shaped(1, 128)], "average"
    )(exchange(solved, "sub"), to_place, from_place, weight)
    inner_far = lax.ppermute(inner_sum, "crs", [(y, y ^ 2) for y in range(4)])
    out, inner = call(unpack_kernel, [VMEM] * 3, [shaped(6, 4, 768), shaped(1, 1)], "unpack")(
        exchange(averaged, "sub"), inner_sum, inner_far
    )
    return out.transpose(1, 0, 2), inner.reshape(1)


def solution(mesh):
    return jax.shard_map(
        body,
        mesh=mesh,
        in_specs=(
            P("sub", None, "crs"),
            P("sub", None, "crs"),
            P("sub", None, "crs"),
            P("sub", None, None, "crs"),
            P("sub", None, None, "crs"),
            P(),
            P("sub", None),
            P("crs", None),
        ),
        out_specs=(P("sub", None, "crs"), P()),
        check_vma=False,
    )
```

```python
import jax
import jax.numpy as jnp
from jax import lax
from jax.experimental import pallas as pl
from jax.experimental.pallas import tpu as pltpu
from jax.sharding import PartitionSpec as P


F32 = jnp.float32
BF16 = jnp.bfloat16
VMEM = pltpu.VMEM
SMEM = pltpu.SMEM
HBM = pltpu.HBM


def iota(shape, axis):
    return lax.broadcasted_iota(jnp.int32, shape, axis)


def pair_transpose(first, second):
    both = jnp.concatenate([first, second], axis=1)
    turned = both.T
    return turned[:64], turned[64:]


def stack_rows(faces, k):
    return jnp.concatenate(
        [
            faces[s][:, p * 192 + k * 64 : p * 192 + k * 64 + 64]
            for s in range(4)
            for p in range(4)
        ],
        axis=0,
    )


def slot_faces(ref, s, pads):
    return jnp.concatenate([ref[f, s : s + 1, :] for f in range(6)] + pads, axis=0)


def unpack_faces(tiles):
    first = jnp.concatenate([tiles[0], tiles[1]], axis=0).T
    second = jnp.concatenate([tiles[2], jnp.zeros_like(tiles[2])], axis=0).T
    faces = []
    for s in range(4):
        pieces = []
        for p in range(4):
            row = s * 32 + p * 8
            pieces += [first[row : row + 8], second[row : row + 8, :64]]
        faces.append(jnp.concatenate(pieces, axis=1))
    return faces


def to_slots(tiles):
    pad = jnp.zeros((64, 32), F32)
    return jnp.concatenate(
        [
            jnp.concatenate([tile[:, s * 32 : s * 32 + 32] for tile in tiles] + [pad], axis=1)
            for s in range(4)
        ],
        axis=0,
    )


def from_slots(rows, k):
    return jnp.concatenate(
        [rows[s * 64 : s * 64 + 64, k * 32 : k * 32 + 32] for s in range(4)], axis=1
    )


def split(values):
    high = values.astype(BF16)
    rest = values - high.astype(F32)
    middle = rest.astype(BF16)
    return high, middle, (rest - middle.astype(F32)).astype(BF16)


def select_rows(onehot, values):
    width = values.shape[1]
    out = jnp.dot(
        onehot, jnp.concatenate(split(values), axis=1), preferred_element_type=F32
    )
    return (out[:, :width] + out[:, width : 2 * width]) + out[:, 2 * width :]


def rows_ahead(values, count):
    return pltpu.roll(values, (-count) % 256, 0)


def lanes_ahead(values, count):
    return pltpu.roll(values, (-count) % values.shape[1], 1)


def step_forward(values, direction):
    row = iota(values.shape, 0)
    if direction == 0:
        return rows_ahead(values, 64)
    if direction == 1:
        return jnp.where(row // 16 % 4 == 3, rows_ahead(values, -48), rows_ahead(values, 16))
    return jnp.where(row % 16 == 15, rows_ahead(values, -15), rows_ahead(values, 1))


def step_back(values, direction):
    row = iota(values.shape, 0)
    if direction == 0:
        return rows_ahead(values, -64)
    if direction == 1:
        return jnp.where(row // 16 % 4 == 0, rows_ahead(values, 48), rows_ahead(values, -16))
    return jnp.where(row % 16 == 0, rows_ahead(values, 15), rows_ahead(values, -1))


def partner(values):
    face = iota(values.shape, 1) % 8
    minus = lanes_ahead(values, 3)
    plus = lanes_ahead(values, -3)
    out = step_forward(minus, 0)
    out = jnp.where(face == 1, step_forward(minus, 1), out)
    out = jnp.where(face == 2, step_forward(minus, 2), out)
    out = jnp.where(face == 3, step_back(plus, 0), out)
    out = jnp.where(face == 4, step_back(plus, 1), out)
    return jnp.where(face == 5, step_back(plus, 2), out)


def fetch(sources, targets, sems):
    copies = [
        pltpu.make_async_copy(source, target, sems.at[at])
        for at, (source, target) in enumerate(zip(sources, targets))
    ]
    for copy in copies:
        copy.start()
    return copies


def pack_kernel(
    assign_hbm, corners_hbm, solid_hbm, residual_hbm, stiffness_hbm, out_ref, solid_ref,
    assign, corners, solid, residual, stiffness, sems,
):
    copies = fetch(
        [assign_hbm, corners_hbm, solid_hbm, residual_hbm, stiffness_hbm],
        [assign, corners, solid, residual, stiffness],
        sems,
    )
    for copy in copies:
        copy.wait()
    first = 4 * lax.axis_index("sub")
    res = []
    stiff = []
    ones = jnp.ones((1, 768), F32)
    for s in range(4):
        vertex = jnp.full((1, 768), corners[s, 0].astype(F32), F32)
        place = jnp.full((1, 768), assign[first + s].astype(F32), F32)
        res.append(slot_faces(residual, s, [vertex, place]))
        stiff.append(slot_faces(stiffness, s, [ones, ones]))
    pairs = [((res, 0), (res, 1)), ((res, 2), (stiff, 0)), ((stiff, 1), (stiff, 2))]
    for at, (one, two) in enumerate(pairs):
        a, b = pair_transpose(stack_rows(*one), stack_rows(*two))
        out_ref[:, 0, at * 256 : at * 256 + 128] = a
        out_ref[:, 0, at * 256 + 128 : at * 256 + 256] = b
    pieces = []
    for s in range(4):
        for p in range(4):
            pieces += [solid[s, p : p + 1, :].astype(F32), jnp.zeros((1, 2), F32)]
    solid_ref[...] = jnp.concatenate(pieces, axis=1)


def weigh_kernel(in_ref, out_ref, weight_ref, place_ref, slot_ref, vertex_ref):
    tiles = [in_ref[:, 0, at * 128 : at * 128 + 128] for at in range(6)]
    res = to_slots(tiles[:3])
    stiff = to_slots(tiles[3:])
    lane = iota((256, 256), 1).astype(F32)
    to_place = jnp.where(res[:, 7:8] == lane, 1.0, 0.0).astype(F32)
    from_place = to_place.astype(BF16)
    to_place = to_place.T.astype(BF16)
    both = select_rows(to_place, jnp.concatenate([res, stiff], axis=1))
    res = both[:, :128]
    stiff = both[:, 128:]
    weight = stiff / (stiff + partner(stiff))
    back = select_rows(from_place, weight * (res + partner(res)))
    for k in range(3):
        out_ref[:, 0, k * 128 : k * 128 + 128] = from_slots(back, k)
    weight_ref[...] = weight
    place_ref[...] = to_place
    slot_ref[...] = from_place
    vertex_ref[...] = jnp.broadcast_to(res[:, 6:7], (256, 128)).T[0:1]


def face_mask(shape, index):
    lane = iota(shape, 1)
    return (lane // 32 == index // 6) & (lane % 8 == index % 6)


def parts_kernel(in_ref, solid_ref, basis, message_ref, rhs):
    patch = iota((64, 128), 1) // 8 % 4
    for k in range(3):
        value = in_ref[:, 0, k * 128 : k * 128 + 128] * solid_ref[...]
        for p in range(4):
            row = p * 192 + k * 64
            rhs[row : row + 64, :] = jnp.where(patch == p, value, 0.0).astype(BF16)
    coarse = jnp.dot(basis[...], rhs[...], preferred_element_type=F32)
    parts = []
    for s in range(4):
        part = jnp.zeros((24, 128), F32)
        for f in range(6):
            at = s * 6 + f
            part = part + jnp.where(face_mask((24, 128), at), coarse[at * 24 : at * 24 + 24], 0.0)
        parts += [part, jnp.zeros((8, 128), F32)]
    row = jnp.sum(jnp.concatenate(parts, axis=0).T, axis=0, keepdims=True)
    message_ref[...] = jnp.broadcast_to(row.reshape(1, 1, 128), message_ref.shape)


STEPS = 2


def solve_kernel(in_ref, solid_ref, rhs, inverses, local_ref, inner_ref):
    step = pl.program_id(0)
    faces = 24 // STEPS

    @pl.when(step == 0)
    def _():
        local_ref[...] = jnp.zeros_like(local_ref)

    product = jnp.dot(inverses[...], rhs[...], preferred_element_type=F32)
    held = local_ref[...]
    for at in range(faces):
        mask = face_mask((192, 128), step * faces + at)
        held = jnp.where(mask, product[at * 192 : at * 192 + 192], held)
    local_ref[...] = held

    @pl.when(step == STEPS - 1)
    def _():
        product_sum = jnp.zeros((64, 128), F32)
        for k in range(3):
            product_sum = product_sum + in_ref[:, 0, k * 128 : k * 128 + 128] * (
                held[k * 64 : k * 64 + 64]
            )
        inner = jnp.sum(
            jnp.sum(product_sum, axis=0, keepdims=True) * solid_ref[...], axis=1, keepdims=True
        )
        inner_ref[...] = jnp.broadcast_to(inner, (1, 128))


def columns_kernel(
    after_ref, inverse_hbm, corners_hbm, basis_hbm, out_ref, basis_ref, inverse, corners, sems
):
    copies = fetch(
        [inverse_hbm, corners_hbm, basis_hbm], [inverse, corners, basis_ref], sems
    )
    lane = iota((1, 128), 1)
    index = jnp.full((1, 128), -1, jnp.int32)
    copies[1].wait()
    for s in range(4):
        for c in range(8):
            first = s * 32 + c * 3
            here = (lane >= first) & (lane < first + 3)
            index = jnp.where(here, 3 * corners[s, c] + lane - first, index)
    wanted = jnp.where(iota((768, 128), 0) == index, 1.0, 0.0).astype(BF16)
    copies[0].wait()
    picked = jnp.dot(
        jnp.concatenate(split(inverse[...]), axis=0), wanted, preferred_element_type=F32
    )
    out_ref[...] = jnp.concatenate([picked[:192], picked[192:384], picked[384:]], axis=1)
    copies[2].wait()


def pick_kernel(after_ref, vertex_ref, own_ref, one_ref, two_ref, three_ref, out_ref, columns):
    for ahead, block_ref in enumerate((own_ref, one_ref, two_ref, three_ref)):
        block = lax.rem(lax.axis_index("crs") + ahead, 4) * 192
        columns[pl.ds(pl.multiple_of(block, 8), 192), :] = block_ref[...]
    parts = columns[...].astype(BF16)
    vertex = 3.0 * jnp.broadcast_to(vertex_ref[...], (128, 256)).T[:, 0:1]
    entry = iota((256, 768), 1).astype(F32)
    for j in range(3):
        rows = jnp.where(entry == vertex + j, 1.0, 0.0).astype(BF16)
        out = jnp.dot(rows, parts, preferred_element_type=F32)
        out_ref[j * 256 : j * 256 + 256, :] = (out[:, :128] + out[:, 128:256]) + out[:, 256:]


def coarse_kernel(
    in_ref, place_ref, picked_ref, local_ref, inner_ref, solid_ref, basis_ref, out_ref
):
    summed = in_ref[0:64, 0, :]
    me = lax.axis_index("sub")
    mine = in_ref[pl.ds(me, 1), 0, :]
    for y in range(1, 4):
        summed = summed + in_ref[y * 64 : y * 64 + 64, 0, :]
        mine = mine + in_ref[pl.ds(y * 64 + me, 1), 0, :]
    parts = jnp.concatenate([summed[:, s * 32 : s * 32 + 32] for s in range(4)], axis=0)
    parts = jnp.concatenate(
        [part.astype(F32) for part in split(parts)] + [jnp.zeros((256, 32), F32)], axis=1
    )
    parts = jnp.dot(place_ref[...], parts.astype(BF16), preferred_element_type=F32)
    parts = (parts + lanes_ahead(parts, 32)) + lanes_ahead(parts, 64)
    for direction, count in ((2, 3), (1, 6), (0, 12)):
        parts = parts + step_back(lanes_ahead(parts, count), direction)
    terms = jnp.zeros((256, 128), F32)
    for j in range(3):
        terms = terms + picked_ref[j * 256 : j * 256 + 256, :] * parts[:, j : j + 1]
    rounded = jnp.sum(terms, axis=0, keepdims=True).astype(BF16).astype(F32)
    inner = jnp.sum(rounded * mine, axis=1, keepdims=True)
    inner = inner_ref[...] + 0.25 * inner
    values = jnp.broadcast_to(rounded, (128, 128)).T
    faces = []
    for s in range(4):
        rows = []
        for f in range(6):
            at = s * 6 + f
            block = basis_ref[at * 24 : at * 24 + 24, :].astype(F32)
            factor = values[s * 32 : s * 32 + 24, 0:1]
            rows.append(jnp.sum(block * factor, axis=0, keepdims=True))
        faces.append(jnp.concatenate(rows + [jnp.zeros((2, 768), F32)], axis=0))
    a, b = pair_transpose(stack_rows(faces, 0), stack_rows(faces, 1))
    c, _ = pair_transpose(stack_rows(faces, 2), jnp.zeros((128, 64), F32))
    for k, tile in enumerate((a, b, c)):
        tile = solid_ref[...] * (local_ref[k * 64 : k * 64 + 64] + tile)
        if k == 0:
            tile = jnp.where(iota((64, 128), 1) == 6, inner, tile)
        out_ref[:, 0, k * 128 : k * 128 + 128] = tile


def average_kernel(in_ref, place_ref, slot_ref, weight_ref, out_ref, inner_ref):
    tiles = [in_ref[:, 0, k * 128 : k * 128 + 128] for k in range(3)]
    inner_ref[...] = jnp.sum(tiles[0], axis=0, keepdims=True)
    values = select_rows(place_ref[...], to_slots(tiles))
    weight = weight_ref[...]
    values = weight * values + (1.0 - weight) * partner(values)
    back = select_rows(slot_ref[...], values)
    for k in range(3):
        out_ref[:, 0, k * 128 : k * 128 + 128] = from_slots(back, k)


def unpack_kernel(in_ref, sum_ref, one_ref, two_ref, three_ref, out_ref, inner_ref):
    inner = (sum_ref[...] + two_ref[...]) + (one_ref[...] + three_ref[...])
    inner_ref[...] = inner[:, 6:7]
    faces = unpack_faces([in_ref[:, 0, k * 128 : k * 128 + 128] for k in range(3)])
    for f in range(6):
        out_ref[f] = jnp.concatenate([faces[s][f : f + 1, :] for s in range(4)], axis=0)


def spec(space=VMEM):
    return pl.BlockSpec(memory_space=space)


def shaped(*shape, dtype=F32):
    return jax.ShapeDtypeStruct(shape, dtype)


def call(kernel, inputs, outputs, name, scratch=(), megabytes=8):
    run = pl.pallas_call(
        kernel,
        in_specs=[spec(space) for space in inputs],
        out_specs=tuple(spec() for _ in outputs),
        out_shape=tuple(outputs),
        scratch_shapes=scratch,
        name=name,
        compiler_params=pltpu.CompilerParams(vmem_limit_bytes=megabytes * 2**20),
    )

    def placed(*values):
        return run(
            *(
                pltpu.with_memory_space_constraint(value, space) if space is HBM else value
                for value, space in zip(values, inputs)
            )
        )

    return placed


def exchange(values, axes):
    return lax.all_to_all(values, axes, 0, 0)


def from_ahead(values, ahead):
    return lax.ppermute(values, "crs", [(y, (y - ahead) % 4) for y in range(4)])


def body(residual, stiffness, solid, inverses, coarse_basis, assign, corners, coarse_inverse):
    basis_rows = coarse_basis.transpose(0, 2, 1, 3).reshape(576, 768)
    dma = pltpu.SemaphoreType.DMA

    packed, solid_row = call(
        pack_kernel,
        [HBM] * 5,
        [shaped(64, 1, 768), shaped(1, 128)],
        "pack",
        [
            SMEM((256,), jnp.int32),
            SMEM((4, 8), jnp.int32),
            VMEM((4, 4, 6), jnp.int32),
            VMEM((6, 4, 768), F32),
            VMEM((6, 4, 768), F32),
            dma((5,)),
        ],
    )(
        assign,
        corners,
        solid.transpose(0, 2, 1),
        residual.transpose(1, 0, 2),
        stiffness.transpose(1, 0, 2),
    )
    own_columns, basis_here = call(
        columns_kernel,
        [VMEM, HBM, HBM, HBM],
        [shaped(192, 384), VMEM((576, 768), BF16)],
        "columns",
        [VMEM((192, 768), F32), SMEM((4, 8), jnp.int32), dma((3,))],
    )(solid_row, coarse_inverse, corners, basis_rows)
    arrived, own_columns, basis_here = lax.optimization_barrier(
        (exchange(packed, "sub"), own_columns, basis_here)
    )
    weighed, weight, to_place, from_place, vertex = call(
        weigh_kernel,
        [VMEM],
        [
            shaped(64, 1, 384),
            shaped(256, 128),
            shaped(256, 256, dtype=BF16),
            shaped(256, 256, dtype=BF16),
            shaped(1, 256),
        ],
        "weigh",
    )(arrived)
    others = [from_ahead(own_columns, k) for k in (1, 2, 3)]
    received = exchange(weighed, "sub")
    message, rhs = call(
        parts_kernel,
        [VMEM] * 3,
        [shaped(256, 1, 128), shaped(768, 128, dtype=BF16)],
        "parts",
    )(received, solid_row, basis_here)
    whole = pl.BlockSpec(memory_space=VMEM)
    rows = 4608 // STEPS
    local, inner_part = pl.pallas_call(
        solve_kernel,
        grid=(STEPS,),
        in_specs=[whole, whole, whole, pl.BlockSpec((rows, 768), lambda i: (i, 0))],
        out_specs=(whole, whole),
        out_shape=(shaped(192, 128), shaped(1, 128)),
        name="solve",
        compiler_params=pltpu.CompilerParams(vmem_limit_bytes=16 * 2**20),
    )(
        received,
        solid_row,
        rhs,
        pltpu.with_memory_space_constraint(inverses.reshape(4608, 768), HBM),
    )
    (picked,) = call(
        pick_kernel, [VMEM] * 6, [shaped(768, 128)], "pick", [VMEM((768, 384), F32)]
    )(rhs, vertex, own_columns, *others)
    (solved,) = call(coarse_kernel, [VMEM] * 7, [shaped(64, 1, 384)], "coarse")(
        exchange(message, ("crs", "sub")),
        to_place,
        picked,
        local,
        inner_part,
        solid_row,
        basis_here,
    )
    averaged, inner_sum = call(
        average_kernel, [VMEM] * 4, [shaped(64, 1, 384), shaped(1, 128)], "average"
    )(exchange(solved, "sub"), to_place, from_place, weight)
    out, inner = call(unpack_kernel, [VMEM] * 5, [shaped(6, 4, 768), shaped(1, 1)], "unpack")(
        exchange(averaged, "sub"), inner_sum, *(from_ahead(inner_sum, k) for k in (1, 2, 3))
    )
    return out.transpose(1, 0, 2), inner.reshape(1)


def solution(mesh):
    return jax.shard_map(
        body,
        mesh=mesh,
        in_specs=(
            P("sub", None, "crs"),
            P("sub", None, "crs"),
            P("sub", None, "crs"),
            P("sub", None, None, "crs"),
            P("sub", None, None, "crs"),
            P(),
            P("sub", None),
            P("crs", None),
        ),
        out_specs=(P("sub", None, "crs"), P()),
        check_vma=False,
    )
```

```python
import jax
import jax.numpy as jnp
from jax import lax
from jax.experimental import pallas as pl
from jax.experimental.pallas import tpu as pltpu
from jax.sharding import PartitionSpec as P


F32 = jnp.float32
BF16 = jnp.bfloat16
VMEM = pltpu.VMEM
SMEM = pltpu.SMEM
HBM = pltpu.HBM


def iota(shape, axis):
    return lax.broadcasted_iota(jnp.int32, shape, axis)


def pair_transpose(first, second):
    both = jnp.concatenate([first, second], axis=1)
    turned = both.T
    return turned[:64], turned[64:]


def stack_rows(faces, k):
    return jnp.concatenate(
        [
            faces[s][:, p * 192 + k * 64 : p * 192 + k * 64 + 64]
            for s in range(4)
            for p in range(4)
        ],
        axis=0,
    )


def slot_faces(ref, s, pads):
    return jnp.concatenate([ref[f, s : s + 1, :] for f in range(6)] + pads, axis=0)


def unpack_faces(tiles):
    first = jnp.concatenate([tiles[0], tiles[1]], axis=0).T
    second = jnp.concatenate([tiles[2], jnp.zeros_like(tiles[2])], axis=0).T
    faces = []
    for s in range(4):
        pieces = []
        for p in range(4):
            row = s * 32 + p * 8
            pieces += [first[row : row + 8], second[row : row + 8, :64]]
        faces.append(jnp.concatenate(pieces, axis=1))
    return faces


def to_slots(tiles):
    pad = jnp.zeros((64, 32), F32)
    return jnp.concatenate(
        [
            jnp.concatenate([tile[:, s * 32 : s * 32 + 32] for tile in tiles] + [pad], axis=1)
            for s in range(4)
        ],
        axis=0,
    )


def from_slots(rows, k):
    return jnp.concatenate(
        [rows[s * 64 : s * 64 + 64, k * 32 : k * 32 + 32] for s in range(4)], axis=1
    )


def split(values):
    high = values.astype(BF16)
    rest = values - high.astype(F32)
    middle = rest.astype(BF16)
    return high, middle, (rest - middle.astype(F32)).astype(BF16)


def select_rows(onehot, values):
    width = values.shape[1]
    out = jnp.dot(
        onehot, jnp.concatenate(split(values), axis=1), preferred_element_type=F32
    )
    return (out[:, :width] + out[:, width : 2 * width]) + out[:, 2 * width :]


def rows_ahead(values, count):
    return pltpu.roll(values, (-count) % 256, 0)


def lanes_ahead(values, count):
    return pltpu.roll(values, (-count) % values.shape[1], 1)


def step_forward(values, direction):
    row = iota(values.shape, 0)
    if direction == 0:
        return rows_ahead(values, 64)
    if direction == 1:
        return jnp.where(row // 16 % 4 == 3, rows_ahead(values, -48), rows_ahead(values, 16))
    return jnp.where(row % 16 == 15, rows_ahead(values, -15), rows_ahead(values, 1))


def step_back(values, direction):
    row = iota(values.shape, 0)
    if direction == 0:
        return rows_ahead(values, -64)
    if direction == 1:
        return jnp.where(row // 16 % 4 == 0, rows_ahead(values, 48), rows_ahead(values, -16))
    return jnp.where(row % 16 == 0, rows_ahead(values, 15), rows_ahead(values, -1))


def partner(values):
    face = iota(values.shape, 1) % 8
    minus = lanes_ahead(values, 3)
    plus = lanes_ahead(values, -3)
    out = step_forward(minus, 0)
    out = jnp.where(face == 1, step_forward(minus, 1), out)
    out = jnp.where(face == 2, step_forward(minus, 2), out)
    out = jnp.where(face == 3, step_back(plus, 0), out)
    out = jnp.where(face == 4, step_back(plus, 1), out)
    return jnp.where(face == 5, step_back(plus, 2), out)


def fetch(sources, targets, sems):
    copies = [
        pltpu.make_async_copy(source, target, sems.at[at])
        for at, (source, target) in enumerate(zip(sources, targets))
    ]
    for copy in copies:
        copy.start()
    return copies


def pack_kernel(
    assign_hbm, corners_hbm, solid_hbm, residual_hbm, stiffness_hbm, out_ref, solid_ref,
    assign, corners, solid, residual, stiffness, sems,
):
    copies = fetch(
        [assign_hbm, corners_hbm, solid_hbm, residual_hbm, stiffness_hbm],
        [assign, corners, solid, residual, stiffness],
        sems,
    )
    for copy in copies:
        copy.wait()
    first = 4 * lax.axis_index("sub")
    res = []
    stiff = []
    ones = jnp.ones((1, 768), F32)
    for s in range(4):
        vertex = jnp.full((1, 768), corners[s, 0].astype(F32), F32)
        place = jnp.full((1, 768), assign[first + s].astype(F32), F32)
        res.append(slot_faces(residual, s, [vertex, place]))
        stiff.append(slot_faces(stiffness, s, [ones, ones]))
    pairs = [((res, 0), (res, 1)), ((res, 2), (stiff, 0)), ((stiff, 1), (stiff, 2))]
    for at, (one, two) in enumerate(pairs):
        a, b = pair_transpose(stack_rows(*one), stack_rows(*two))
        out_ref[:, 0, at * 256 : at * 256 + 128] = a
        out_ref[:, 0, at * 256 + 128 : at * 256 + 256] = b
    pieces = []
    for s in range(4):
        for p in range(4):
            pieces += [solid[s, p : p + 1, :].astype(F32), jnp.zeros((1, 2), F32)]
    solid_ref[...] = jnp.concatenate(pieces, axis=1)


def weigh_kernel(in_ref, place_ref, slot_ref, out_ref, weight_ref, vertex_ref):
    tiles = [in_ref[:, 0, at * 128 : at * 128 + 128] for at in range(6)]
    res = to_slots(tiles[:3])
    stiff = to_slots(tiles[3:])
    both = select_rows(place_ref[...], jnp.concatenate([res, stiff], axis=1))
    res = both[:, :128]
    stiff = both[:, 128:]
    weight = stiff / (stiff + partner(stiff))
    back = select_rows(slot_ref[...], weight * (res + partner(res)))
    for k in range(3):
        out_ref[:, 0, k * 128 : k * 128 + 128] = from_slots(back, k)
    weight_ref[...] = weight
    vertex_ref[...] = jnp.broadcast_to(res[:, 6:7], (256, 128)).T[0:1]


def face_mask(shape, index):
    lane = iota(shape, 1)
    return (lane // 32 == index // 6) & (lane % 8 == index % 6)


def parts_kernel(in_ref, solid_ref, basis, message_ref, rhs):
    patch = iota((64, 128), 1) // 8 % 4
    for k in range(3):
        value = in_ref[:, 0, k * 128 : k * 128 + 128] * solid_ref[...]
        for p in range(4):
            row = p * 192 + k * 64
            rhs[row : row + 64, :] = jnp.where(patch == p, value, 0.0).astype(BF16)
    coarse = jnp.dot(basis[...], rhs[...], preferred_element_type=F32)
    parts = []
    for s in range(4):
        part = jnp.zeros((24, 128), F32)
        for f in range(6):
            at = s * 6 + f
            part = part + jnp.where(face_mask((24, 128), at), coarse[at * 24 : at * 24 + 24], 0.0)
        parts += [part, jnp.zeros((8, 128), F32)]
    row = jnp.sum(jnp.concatenate(parts, axis=0).T, axis=0, keepdims=True)
    message_ref[...] = jnp.broadcast_to(row.reshape(1, 1, 128), message_ref.shape)


STEPS = 2


def solve_kernel(in_ref, solid_ref, rhs, inverses, local_ref, inner_ref):
    step = pl.program_id(0)
    faces = 24 // STEPS

    @pl.when(step == 0)
    def _():
        local_ref[...] = jnp.zeros_like(local_ref)

    product = jnp.dot(inverses[...], rhs[...], preferred_element_type=F32)
    held = local_ref[...]
    for at in range(faces):
        mask = face_mask((192, 128), step * faces + at)
        held = jnp.where(mask, product[at * 192 : at * 192 + 192], held)
    local_ref[...] = held

    @pl.when(step == STEPS - 1)
    def _():
        product_sum = jnp.zeros((64, 128), F32)
        for k in range(3):
            product_sum = product_sum + in_ref[:, 0, k * 128 : k * 128 + 128] * (
                held[k * 64 : k * 64 + 64]
            )
        inner = jnp.sum(
            jnp.sum(product_sum, axis=0, keepdims=True) * solid_ref[...], axis=1, keepdims=True
        )
        inner_ref[...] = jnp.broadcast_to(inner, (1, 128))


def columns_kernel(
    after_ref, inverse_hbm, corners_hbm, basis_hbm, assign_hbm, out_ref, basis_ref, place_ref,
    slot_ref, inverse, corners, assign, sems,
):
    copies = fetch(
        [inverse_hbm, corners_hbm, basis_hbm, assign_hbm],
        [inverse, corners, basis_ref, assign],
        sems,
    )
    copies[3].wait()
    row = iota((256, 256), 0)
    column = iota((256, 256), 1)
    by_slot = jnp.where(row == assign[...], 1.0, 0.0).astype(BF16)
    order = jnp.where(row == 4 * (column % 64) + column // 64, 1.0, 0.0).astype(BF16)
    to_place = jnp.dot(by_slot, order, preferred_element_type=F32)
    place_ref[...] = to_place.astype(BF16)
    slot_ref[...] = to_place.T.astype(BF16)
    lane = iota((1, 128), 1)
    index = jnp.full((1, 128), -1, jnp.int32)
    copies[1].wait()
    for s in range(4):
        for c in range(8):
            first = s * 32 + c * 3
            here = (lane >= first) & (lane < first + 3)
            index = jnp.where(here, 3 * corners[s, c] + lane - first, index)
    wanted = jnp.where(iota((768, 128), 0) == index, 1.0, 0.0).astype(BF16)
    copies[0].wait()
    picked = jnp.dot(
        jnp.concatenate(split(inverse[...]), axis=0), wanted, preferred_element_type=F32
    )
    out_ref[...] = jnp.concatenate([picked[:192], picked[192:384], picked[384:]], axis=1)
    copies[2].wait()


def pick_kernel(after_ref, vertex_ref, own_ref, one_ref, two_ref, three_ref, out_ref, columns):
    for ahead, block_ref in enumerate((own_ref, one_ref, two_ref, three_ref)):
        block = lax.rem(lax.axis_index("crs") + ahead, 4) * 192
        columns[pl.ds(pl.multiple_of(block, 8), 192), :] = block_ref[...]
    parts = columns[...].astype(BF16)
    vertex = 3.0 * jnp.broadcast_to(vertex_ref[...], (128, 256)).T[:, 0:1]
    entry = iota((256, 768), 1).astype(F32)
    for j in range(3):
        rows = jnp.where(entry == vertex + j, 1.0, 0.0).astype(BF16)
        out = jnp.dot(rows, parts, preferred_element_type=F32)
        out_ref[j * 256 : j * 256 + 256, :] = (out[:, :128] + out[:, 128:256]) + out[:, 256:]


def coarse_kernel(
    in_ref, place_ref, picked_ref, local_ref, inner_ref, solid_ref, basis_ref, out_ref
):
    summed = in_ref[0:64, 0, :]
    me = lax.axis_index("sub")
    mine = in_ref[pl.ds(me, 1), 0, :]
    for y in range(1, 4):
        summed = summed + in_ref[y * 64 : y * 64 + 64, 0, :]
        mine = mine + in_ref[pl.ds(y * 64 + me, 1), 0, :]
    parts = jnp.concatenate([summed[:, s * 32 : s * 32 + 32] for s in range(4)], axis=0)
    parts = jnp.concatenate(
        [part.astype(F32) for part in split(parts)] + [jnp.zeros((256, 32), F32)], axis=1
    )
    parts = jnp.dot(place_ref[...], parts.astype(BF16), preferred_element_type=F32)
    parts = (parts + lanes_ahead(parts, 32)) + lanes_ahead(parts, 64)
    for direction, count in ((2, 3), (1, 6), (0, 12)):
        parts = parts + step_back(lanes_ahead(parts, count), direction)
    terms = jnp.zeros((256, 128), F32)
    for j in range(3):
        terms = terms + picked_ref[j * 256 : j * 256 + 256, :] * parts[:, j : j + 1]
    rounded = jnp.sum(terms, axis=0, keepdims=True).astype(BF16).astype(F32)
    inner = jnp.sum(rounded * mine, axis=1, keepdims=True)
    inner = inner_ref[...] + 0.25 * inner
    values = jnp.broadcast_to(rounded, (128, 128)).T
    faces = []
    for s in range(4):
        rows = []
        for f in range(6):
            at = s * 6 + f
            block = basis_ref[at * 24 : at * 24 + 24, :].astype(F32)
            factor = values[s * 32 : s * 32 + 24, 0:1]
            rows.append(jnp.sum(block * factor, axis=0, keepdims=True))
        faces.append(jnp.concatenate(rows + [jnp.zeros((2, 768), F32)], axis=0))
    a, b = pair_transpose(stack_rows(faces, 0), stack_rows(faces, 1))
    c, _ = pair_transpose(stack_rows(faces, 2), jnp.zeros((128, 64), F32))
    for k, tile in enumerate((a, b, c)):
        tile = solid_ref[...] * (local_ref[k * 64 : k * 64 + 64] + tile)
        if k == 0:
            tile = jnp.where(iota((64, 128), 1) == 6, inner, tile)
        out_ref[:, 0, k * 128 : k * 128 + 128] = tile


def average_kernel(in_ref, place_ref, slot_ref, weight_ref, out_ref, inner_ref):
    tiles = [in_ref[:, 0, k * 128 : k * 128 + 128] for k in range(3)]
    inner_ref[...] = jnp.sum(tiles[0], axis=0, keepdims=True)
    values = select_rows(place_ref[...], to_slots(tiles))
    weight = weight_ref[...]
    values = weight * values + (1.0 - weight) * partner(values)
    back = select_rows(slot_ref[...], values)
    for k in range(3):
        out_ref[:, 0, k * 128 : k * 128 + 128] = from_slots(back, k)


def unpack_kernel(in_ref, sum_ref, one_ref, two_ref, three_ref, out_ref, inner_ref):
    inner = (sum_ref[...] + two_ref[...]) + (one_ref[...] + three_ref[...])
    inner_ref[...] = inner[:, 6:7]
    faces = unpack_faces([in_ref[:, 0, k * 128 : k * 128 + 128] for k in range(3)])
    for f in range(6):
        out_ref[f] = jnp.concatenate([faces[s][f : f + 1, :] for s in range(4)], axis=0)


def spec(space=VMEM):
    return pl.BlockSpec(memory_space=space)


def shaped(*shape, dtype=F32):
    return jax.ShapeDtypeStruct(shape, dtype)


def call(kernel, inputs, outputs, name, scratch=(), megabytes=8):
    run = pl.pallas_call(
        kernel,
        in_specs=[spec(space) for space in inputs],
        out_specs=tuple(spec() for _ in outputs),
        out_shape=tuple(outputs),
        scratch_shapes=scratch,
        name=name,
        compiler_params=pltpu.CompilerParams(vmem_limit_bytes=megabytes * 2**20),
    )

    def placed(*values):
        return run(
            *(
                pltpu.with_memory_space_constraint(value, space) if space is HBM else value
                for value, space in zip(values, inputs)
            )
        )

    return placed


def exchange(values, axes):
    return lax.all_to_all(values, axes, 0, 0)


def from_ahead(values, ahead):
    return lax.ppermute(values, "crs", [(y, (y - ahead) % 4) for y in range(4)])


def body(residual, stiffness, solid, inverses, coarse_basis, assign, corners, coarse_inverse):
    basis_rows = coarse_basis.transpose(0, 2, 1, 3).reshape(576, 768)
    dma = pltpu.SemaphoreType.DMA

    packed, solid_row = call(
        pack_kernel,
        [HBM] * 5,
        [shaped(64, 1, 768), shaped(1, 128)],
        "pack",
        [
            SMEM((256,), jnp.int32),
            SMEM((4, 8), jnp.int32),
            VMEM((4, 4, 6), jnp.int32),
            VMEM((6, 4, 768), F32),
            VMEM((6, 4, 768), F32),
            dma((5,)),
        ],
    )(
        assign,
        corners,
        solid.transpose(0, 2, 1),
        residual.transpose(1, 0, 2),
        stiffness.transpose(1, 0, 2),
    )
    own_columns, basis_here, to_place, from_place = call(
        columns_kernel,
        [VMEM, HBM, HBM, HBM, HBM],
        [
            shaped(192, 384),
            VMEM((576, 768), BF16),
            VMEM((256, 256), BF16),
            VMEM((256, 256), BF16),
        ],
        "columns",
        [VMEM((192, 768), F32), SMEM((4, 8), jnp.int32), VMEM((1, 256), jnp.int32), dma((4,))],
    )(solid_row, coarse_inverse, corners, basis_rows, assign.reshape(1, 256))
    arrived, own_columns, basis_here, to_place, from_place = lax.optimization_barrier(
        (exchange(packed, "sub"), own_columns, basis_here, to_place, from_place)
    )
    weighed, weight, vertex = call(
        weigh_kernel,
        [VMEM] * 3,
        [shaped(64, 1, 384), shaped(256, 128), shaped(1, 256)],
        "weigh",
    )(arrived, to_place, from_place)
    others = [from_ahead(own_columns, k) for k in (1, 2, 3)]
    received = exchange(weighed, "sub")
    message, rhs = call(
        parts_kernel,
        [VMEM] * 3,
        [shaped(256, 1, 128), shaped(768, 128, dtype=BF16)],
        "parts",
    )(received, solid_row, basis_here)
    whole = pl.BlockSpec(memory_space=VMEM)
    rows = 4608 // STEPS
    local, inner_part = pl.pallas_call(
        solve_kernel,
        grid=(STEPS,),
        in_specs=[whole, whole, whole, pl.BlockSpec((rows, 768), lambda i: (i, 0))],
        out_specs=(whole, whole),
        out_shape=(shaped(192, 128), shaped(1, 128)),
        name="solve",
        compiler_params=pltpu.CompilerParams(vmem_limit_bytes=16 * 2**20),
    )(
        received,
        solid_row,
        rhs,
        pltpu.with_memory_space_constraint(inverses.reshape(4608, 768), HBM),
    )
    (picked,) = call(
        pick_kernel, [VMEM] * 6, [shaped(768, 128)], "pick", [VMEM((768, 384), F32)]
    )(rhs, vertex, own_columns, *others)
    (solved,) = call(coarse_kernel, [VMEM] * 7, [shaped(64, 1, 384)], "coarse")(
        exchange(message, ("crs", "sub")),
        to_place,
        picked,
        local,
        inner_part,
        solid_row,
        basis_here,
    )
    averaged, inner_sum = call(
        average_kernel, [VMEM] * 4, [shaped(64, 1, 384), shaped(1, 128)], "average"
    )(exchange(solved, "sub"), to_place, from_place, weight)
    out, inner = call(unpack_kernel, [VMEM] * 5, [shaped(6, 4, 768), shaped(1, 1)], "unpack")(
        exchange(averaged, "sub"), inner_sum, *(from_ahead(inner_sum, k) for k in (1, 2, 3))
    )
    return out.transpose(1, 0, 2), inner.reshape(1)


def solution(mesh):
    return jax.shard_map(
        body,
        mesh=mesh,
        in_specs=(
            P("sub", None, "crs"),
            P("sub", None, "crs"),
            P("sub", None, "crs"),
            P("sub", None, None, "crs"),
            P("sub", None, None, "crs"),
            P(),
            P("sub", None),
            P("crs", None),
        ),
        out_specs=(P("sub", None, "crs"), P()),
        check_vma=False,
    )
```
